512 devices in a mesh: ctx: 16 (over z_lo, core), head: 32 (over z_hi, y, x).
Axes of the slice: x: 4, y: 4, z: 16 (z_hi: 2, z_lo: 8; z = z_hi * 8 + z_lo), core: 2. Of those that a mesh axis runs over, the one named last changes fastest.
Arguments:
- tokens: bfloat16 [4096, 4096], P('ctx', 'head'), may hold values from -6 to 6
- qkv_weight: bfloat16 [4096, 3, 4096], P(None, None, 'head'), may hold values from -0.09375 to 0.09375
- out_weight: bfloat16 [4096, 4096], P('head'), may hold values from -1 to 1
- signs: int32 [32, 2, 128], P('head'), may hold values from 0 to 1
- rows: int32 [32, 2, 64], P('head'), may hold values from 0 to 127
Outputs:
- mixed: bfloat16 [4096, 4096], P('ctx', 'head')
The draws below stay inside these ranges and needn't reach their ends.
Inputs may be any that keep to these rules, and one draw needn't show every extreme that they name: `signs`: each sign bit s gives the sign 2 s - 1. `rows`: rows are drawn with repetition.
All inputs are finite; a program needn't handle non-finite values.
Results may differ from the reference program's by a relative error of at most 0.025.
Values may be sent and summed in bfloat16 or wider, within the bound.
A program may use at most 128 MiB of HBM per device.

```python
import math
import jax
import jax.numpy as jnp
from jax import lax

D = 4096
H = 32
HD = 128
M = 64
BLOCK = 256
TOKENS = 4096


def place_ends(result, rng, low, largest):
    longest = result.shape.index(max(result.shape))
    spots = []
    for shift in (0, 1):
        where = [jax.random.randint(jax.random.fold_in(rng, axis), (), 0, length) for axis, length in enumerate(result.shape)]
        where[longest] = (where[longest] + shift) % result.shape[longest]
        spots.append(tuple(where))
    return result.at[spots[0]].set(low).at[spots[1]].set(largest)


def strengthened(values, key, source, target, blocks, factor):
    owner, partner = [(jnp.arange(values.shape[axis_at]) // (values.shape[axis_at] // blocks)).reshape([-1 if axis == axis_at else 1 for axis in range(values.ndim)]) for axis_at in (source, target)]
    chosen = jax.random.permutation(key, blocks)[partner]
    strong = (owner == chosen) | (owner == (partner + blocks // 2) % blocks)
    return jnp.where(strong, factor * values, values)


def steps_of(stream_key, extent, shards, low, high):
    loudness, own = 1.0, jax.random.fold_in(stream_key, 6)
    for axis_at, parts in shards:
        steps = jnp.exp(jax.random.uniform(jax.random.fold_in(own, axis_at), (parts,), jnp.float32, low / len(shards), high / len(shards)))
        loudness = loudness * jnp.repeat(steps, extent[axis_at] // parts).reshape([-1 if axis == axis_at else 1 for axis in range(len(extent))])
    return loudness


def centred(own_key, shape, deviation, bound, pieces=(), held_as=jnp.bfloat16):
    result = jax.random.normal(own_key, shape, jnp.float32) * deviation
    if len(pieces) > 0:
        result = steps_of(own_key, shape, pieces, -0.22, 0.18) * result
    return jnp.clip(result, min=-bound, max=bound).astype(held_as)


def noise_with(rng, dims, spread, reach, cuts, heavy, kind=jnp.bfloat16):
    entries = spread * jax.random.normal(rng, dims, jnp.float32)
    if cuts:
        entries = entries * steps_of(rng, dims, cuts, -0.22, 0.18)
    return jnp.clip(strengthened(entries, jax.random.fold_in(rng, 3), *heavy), -reach, reach).astype(kind)


def setup_inputs(seed: int = 0) -> dict:
    keys = jax.random.split(jax.random.key(seed), 6)
    return {
        "tokens": centred(keys[0], (TOKENS, D), 1.0, 6.0, ((0, 16), (1, 32))),
        "qkv_weight": centred(keys[1], (D, 3, H * HD), D ** -0.5, 0.09375, ((2, 32),)),
        "out_weight": noise_with(keys[2], (H * HD, D), HD ** -0.5, 1.0, ((0, 32),), (0, 1, 32, 2.75)),
        "signs": place_ends(jax.random.randint(keys[3], (H, 2, HD), 0, 2), jax.random.fold_in(keys[3], 1), 0, 1).astype(jnp.int32),
        "rows": place_ends(jax.random.randint(keys[4], (H, 2, M), 0, HD), jax.random.fold_in(keys[4], 1), 0, HD - 1).astype(jnp.int32),
    }


score_scale = 2.0

def hadamard_table(size_hd):
    row_index = jnp.arange(size_hd, dtype=jnp.int32)[:, None]
    col_index = jnp.arange(size_hd, dtype=jnp.int32)[None, :]
    common = jnp.bitwise_and(row_index, col_index)
    parity = jnp.zeros((size_hd, size_hd), jnp.int32)
    for bit_place in range(size_hd.bit_length() - 1):
        parity = parity + jnp.bitwise_and(jnp.right_shift(common, bit_place), 1)
    return 1.0 - 2.0 * jnp.bitwise_and(parity, 1).astype(jnp.float32)

def sketch_matrix(signs, rows):
    size_hd = signs.shape[-1]
    hadamard = hadamard_table(size_hd)
    selector = (jnp.arange(size_hd, dtype=jnp.int32)[:, None] == rows[..., None, :]).astype(jnp.float32)
    columns = jnp.einsum('de,kief->kidf', hadamard, selector, precision=lax.Precision.HIGHEST)
    signed = (2 * signs - 1).astype(jnp.float32)
    return (signed[..., None] * columns).astype(jnp.bfloat16)

def normalize(raw_rows):
    scale_rows = lax.rsqrt(lax.optimization_barrier(jnp.mean(raw_rows * raw_rows, axis=-1, keepdims=True)) + 1e-06)
    return (raw_rows * scale_rows).astype(jnp.bfloat16)

def features(normed, sketch):
    branches = jnp.einsum('td,idm->tim', normed.astype(jnp.float32), sketch.astype(jnp.float32), precision=lax.Precision.HIGHEST)
    factor = score_scale * score_scale / (HD * math.sqrt(M))
    sketched = factor * branches[:, 0, :] * branches[:, 1, :]
    squared = sketched[:, :, None] * sketched[:, None, :]
    return squared.reshape(sketched.shape[0], M * M).astype(jnp.bfloat16)

def one_head(items):
    head_proj, sketch = items
    length = head_proj.shape[0]
    normed_queries = normalize(head_proj[:, 0])
    normed_keys = normalize(head_proj[:, 1])
    values = head_proj[:, 2].astype(jnp.bfloat16)
    query_feats = features(normed_queries, sketch)
    key_feats = features(normed_keys, sketch)
    nblocks = length // BLOCK
    qf = query_feats.reshape(nblocks, BLOCK, M * M).astype(jnp.float32)
    kf = key_feats.reshape(nblocks, BLOCK, M * M).astype(jnp.float32)
    vbk = values.reshape(nblocks, BLOCK, HD).astype(jnp.float32)
    block_states = jnp.einsum('btf,btd->bfd', kf, vbk, precision=lax.Precision.HIGHEST)
    block_sums = lax.optimization_barrier(jnp.sum(kf, axis=1))
    state_run = jnp.cumsum(block_states, axis=0)
    sum_run = jnp.cumsum(block_sums, axis=0)
    prefix_state = jnp.concatenate([jnp.zeros((1, M * M, HD), jnp.float32), state_run[:-1]], axis=0)
    prefix_sum = jnp.concatenate([jnp.zeros((1, M * M), jnp.float32), sum_run[:-1]], axis=0)
    prefix_state = prefix_state.astype(jnp.bfloat16).astype(jnp.float32)
    prefix_sum = prefix_sum.astype(jnp.bfloat16).astype(jnp.float32)
    num_state = jnp.einsum('btf,bfd->btd', qf, prefix_state, precision=lax.Precision.HIGHEST)
    den_state = jnp.einsum('btf,bf->bt', qf, prefix_sum, precision=lax.Precision.HIGHEST)
    qblk = normed_queries.reshape(nblocks, BLOCK, HD).astype(jnp.float32)
    kblk = normed_keys.reshape(nblocks, BLOCK, HD).astype(jnp.float32)
    scores = jnp.einsum('btd,bpd->btp', qblk, kblk, precision=lax.Precision.HIGHEST)
    causal = (jnp.arange(BLOCK, dtype=jnp.int32)[:, None] >= jnp.arange(BLOCK, dtype=jnp.int32)[None, :]).astype(jnp.float32)
    weights = (score_scale * scores / HD) ** 4 * causal[None]
    den_diag = lax.optimization_barrier(jnp.sum(weights, axis=-1))
    weights_b = weights.astype(jnp.bfloat16).astype(jnp.float32)
    num_diag = jnp.einsum('btp,bpd->btd', weights_b, vbk, precision=lax.Precision.HIGHEST)
    attended = (num_diag + num_state) / (1.0 + den_diag + den_state)[..., None]
    return attended.astype(jnp.bfloat16).reshape(length, HD)

def reference(tokens, qkv_weight, out_weight, signs, rows):
    length = tokens.shape[0]
    projected = jnp.dot(tokens, qkv_weight.reshape(D, 3 * H * HD), preferred_element_type=jnp.float32)
    projected = projected.reshape(length, 3, H, HD).transpose(2, 0, 1, 3)
    sketch = sketch_matrix(signs, rows)
    heads_out = lax.map(one_head, (projected, sketch))
    attended = heads_out.transpose(1, 0, 2).reshape(length, H * HD)
    return jnp.dot(attended, out_weight, preferred_element_type=jnp.float32).astype(jnp.bfloat16)
```

```python
import math

import jax
import jax.numpy as jnp
from jax import lax
from jax.experimental import pallas as pl
from jax.experimental.pallas import tpu as pltpu
from jax.sharding import PartitionSpec as P

MESH = pl.DeviceIdType.MESH
BLOCK = 256
HALF = 128
QUARTER = 64
HD = 128
RING = 4
SHIFTS = (0, 3, 1, 2)

score_scale = 2.0


def hadamard_table(size_hd):
    row_index = jnp.arange(size_hd, dtype=jnp.int32)[:, None]
    col_index = jnp.arange(size_hd, dtype=jnp.int32)[None, :]
    common = jnp.bitwise_and(row_index, col_index)
    parity = jnp.zeros((size_hd, size_hd), jnp.int32)
    for bit_place in range(size_hd.bit_length() - 1):
        parity = parity + jnp.bitwise_and(jnp.right_shift(common, bit_place), 1)
    return 1.0 - 2.0 * jnp.bitwise_and(parity, 1).astype(jnp.float32)


def sketch_matrix(signs, rows):
    size_hd = signs.shape[-1]
    hadamard = hadamard_table(size_hd)
    selector = (jnp.arange(size_hd, dtype=jnp.int32)[:, None] == rows[..., None, :]).astype(
        jnp.float32
    )
    columns = jnp.einsum("de,kief->kidf", hadamard, selector, precision=lax.Precision.HIGHEST)
    signed = (2 * signs - 1).astype(jnp.float32)
    return (signed[..., None] * columns).astype(jnp.bfloat16)


def dot(left, right):
    return jnp.dot(left, right, preferred_element_type=jnp.float32)


def dot_t(left, right):
    return lax.dot_general(left, right, (((1,), (1,)), ((), ())), preferred_element_type=jnp.float32)


def turn(place, step):
    return lax.rem(place + step, RING)


def kernel(
    x_ref, w_ref, wo_ref, sk_ref, out_ref,
    xbuf, wv, wov, acc, vb, fb, qf, num, wsum,
    s1, r1, s2, r2, s3, r3, t1,
    load_sem, z_send, z_recv, ag_send, ag_recv,
    kv_send, kv_pass, kv_recv, rs1_send, rs1_recv, rs2_send, rs2_recv, rs3_send, rs3_recv,
):
    head = lax.axis_index("head")
    ctx = lax.axis_index("ctx")
    chips = lax.axis_size("ctx") // 2
    z = lax.div(head, RING * RING)
    y = lax.rem(lax.div(head, RING), RING)
    x = lax.rem(head, RING)
    zl = lax.div(ctx, 2)
    core = lax.rem(ctx, 2)
    other_core = ctx + 1 - 2 * core
    z_partner = (1 - z) * RING * RING + y * RING + x
    sent = []

    def remote(src, dst, send_sem, recv_sem, **device):
        return pltpu.make_async_remote_copy(
            src_ref=src, dst_ref=dst, send_sem=send_sem, recv_sem=recv_sem,
            device_id=device, device_id_type=MESH,
        )

    def head_at(zz, eta, a, b, first_is_y):
        if first_is_y:
            return zz * RING * RING + a * RING + b
        return zz * RING * RING + b * RING + a

    own_block = xbuf.at[:, pl.ds(pl.multiple_of(head * HD, HD), HD)]
    load_x = pltpu.make_async_copy(x_ref, own_block, load_sem.at[0])
    load_w = pltpu.make_async_copy(w_ref, wv, load_sem.at[1])
    load_wo = pltpu.make_async_copy(wo_ref, wov, load_sem.at[2])
    load_x.start()
    load_w.start()
    load_wo.start()
    barrier = pltpu.get_barrier_semaphore()
    for step in (1, 2, 3):
        for place in (z * 16 + y * RING + turn(x, step), z * 16 + turn(y, step) * RING + x):
            pl.semaphore_signal(barrier, inc=1, device_id={"head": place}, device_id_type=MESH)
    pl.semaphore_signal(barrier, inc=1, device_id={"head": z_partner}, device_id_type=MESH)
    pl.semaphore_signal(barrier, inc=1, device_id={"ctx": other_core}, device_id_type=MESH)

    @pl.when(zl > 0)
    def _():
        pl.semaphore_signal(barrier, inc=1, device_id={"ctx": ctx - 2}, device_id_type=MESH)

    @pl.when(zl < chips - 1)
    def _():
        pl.semaphore_signal(barrier, inc=1, device_id={"ctx": ctx + 2}, device_id_type=MESH)

    acc[...] = jnp.zeros_like(acc)
    pl.semaphore_wait(barrier, 8 + lax.min(zl, 1) + lax.min(chips - 1 - zl, 1))

    load_x.wait()

    z_copy = remote(own_block, own_block, z_send, z_recv, head=z_partner)
    z_copy.start()
    sent.append(z_copy)

    def line(stage, eta, phase, shift):
        first_is_y = eta == 1
        a, b = (y, x) if first_is_y else (x, y)
        zz = z if stage == 0 else 1 - z
        base = (stage * 2 + eta) * 20 + (0 if phase == 0 else 4 + 4 * shift)
        pos = a if phase == 0 else b

        def device(place):
            return head_at(z, eta, place, b, first_is_y) if phase == 0 else head_at(z, eta, a, place, first_is_y)

        def piece(place, low, count):
            if phase == 0:
                t = head_at(zz, eta, place, b, first_is_y)
            else:
                t = head_at(zz, eta, turn(a, SHIFTS[shift]), place, first_is_y)
            return xbuf.at[pl.ds(eta * HALF + low, count), pl.ds(pl.multiple_of(t * HD, HD), HD)]

        def copy(k, what, step):
            return remote(what, what, ag_send.at[base + k], ag_recv.at[base + k], head=device(turn(pos, step)))

        def send(k, what, step):
            one = copy(k, what, step)
            one.start()
            sent.append(one)

        def start():
            send(0, piece(pos, 0, HALF), 1)
            send(1, piece(pos, 0, HALF), 3)

        def relay(side):
            if side == 0:
                copy(0, piece(turn(pos, 3), 0, HALF), 1).wait_recv()
                send(2, piece(turn(pos, 3), 0, QUARTER), 1)
            else:
                copy(1, piece(turn(pos, 1), 0, HALF), 3).wait_recv()
                send(3, piece(turn(pos, 1), QUARTER, QUARTER), 3)

        def finish():
            copy(2, piece(turn(pos, 2), 0, QUARTER), 1).wait_recv()
            copy(3, piece(turn(pos, 2), QUARTER, QUARTER), 3).wait_recv()

        return start, relay, finish

    def spread(stage, filler):
        first = [line(stage, eta, 0, 0) for eta in (0, 1)]
        second = [[line(stage, eta, 1, shift) for shift in range(4)] for eta in (0, 1)]
        for eta in (0, 1):
            first[eta][0]()
        for eta in (0, 1):
            second[eta][0][0]()
        filler()
        for side in (0, 1):
            for eta in (0, 1):
                first[eta][1](side)
                second[eta][1 + side][0]()
        for eta in (0, 1):
            for side in (0, 1):
                second[eta][0][1](side)
        for eta in (0, 1):
            first[eta][2]()
            second[eta][3][0]()
        for shift in (1, 2, 3):
            for side in (0, 1):
                for eta in (0, 1):
                    second[eta][shift][1](side)
        for shift in range(4):
            for eta in (0, 1):
                second[eta][shift][2]()

    chunk = 4 * HD

    def project(zz):
        def one(k, carry):
            low = pl.multiple_of(zz * (16 * HD) + k * chunk, chunk)
            acc[...] += dot(xbuf[:, pl.ds(low, chunk)], wv[pl.ds(low, chunk), :])
            return carry

        lax.fori_loop(0, 4, one, 0)

    spread(0, lambda: None)
    load_w.wait()
    z_block = xbuf.at[:, pl.ds(pl.multiple_of(z_partner * HD, HD), HD)]
    remote(z_block, z_block, z_send, z_recv, head=z_partner).wait_recv()
    spread(1, lambda: project(z))
    project(1 - z)

    def normalize(raw):
        return (raw * lax.rsqrt(jnp.mean(raw * raw, axis=-1, keepdims=True) + 1e-06)).astype(jnp.bfloat16)

    factor = score_scale * score_scale / (HD * math.sqrt(QUARTER))

    def twice(normed):
        return factor * dot(normed, sk_ref[0]) * dot(normed, sk_ref[1])

    kn = normalize(acc[:, HD : 2 * HD])
    kf = twice(kn)
    low_half = lax.broadcasted_iota(jnp.int32, (HALF, HD), 1) < QUARTER
    fb[ctx] = jnp.where(low_half, kf[:HALF], kf[HALF:]).astype(jnp.bfloat16)
    vb[ctx] = acc[:, 2 * HD :].astype(jnp.bfloat16)
    qn = normalize(acc[:, :HD])
    qd = twice(qn)
    lanes_low = lax.broadcasted_iota(jnp.int32, (BLOCK, HD), 1) < QUARTER
    qf[0] = jnp.where(lanes_low, qd, 0.0).astype(jnp.bfloat16)
    qf[1] = jnp.where(lanes_low, 0.0, qd).astype(jnp.bfloat16)

    def kv(slot, sems, offset, target):
        return (
            remote(vb.at[slot], vb.at[slot], sems.at[2 * slot], kv_recv.at[2 * slot], ctx=target),
            remote(fb.at[slot], fb.at[slot], sems.at[2 * slot + 1], kv_recv.at[2 * slot + 1], ctx=target),
        )

    def up(slot):
        return kv(slot, kv_send, 0, ctx + 2)

    def over(slot):
        return kv(slot, kv_pass, 0, other_core)

    def arrive(slot):
        for one in kv(slot, kv_pass, 0, other_core):
            one.wait_recv()

    @pl.when(zl < chips - 1)
    def _():
        for one in up(ctx):
            one.start()

    @pl.when(core == 0)
    def _():
        for one in over(ctx):
            one.start()

    scores = dot_t(qn, kn)
    causal = (
        lax.broadcasted_iota(jnp.int32, (BLOCK, BLOCK), 0)
        >= lax.broadcasted_iota(jnp.int32, (BLOCK, BLOCK), 1)
    )
    scaled = scores * (score_scale / HD)
    square = scaled * scaled
    weights = jnp.where(causal, square * square, 0.0)
    wsum[...] = weights[:, :HD] + weights[:, HD:]
    num[...] = dot(weights.astype(jnp.bfloat16), vb[ctx])

    def attend(slot):
        packed = fb[slot]
        left = dot_t(qf[0], packed)
        right = dot_t(qf[1], packed)
        left = left * left
        right = right * right
        wsum[...] += left + right
        both = jnp.concatenate([left.astype(jnp.bfloat16), right.astype(jnp.bfloat16)], axis=1)
        num[...] += dot(both, vb[slot])

    @pl.when(core == 1)
    def _():
        arrive(2 * zl)
        attend(2 * zl)

    def earlier(s, carry):
        chip = zl - 1 - s
        slot = 2 * chip + core
        arrive(slot)

        @pl.when(zl < chips - 1)
        def _():
            for one in up(slot):
                one.start()

        for one in over(slot):
            one.start()
        attend(slot)
        second = 2 * chip + 1 - core
        arrive(second)
        attend(second)
        return carry

    lax.fori_loop(0, zl, earlier, 0)

    total = 1.0 + jnp.sum(wsum[...], axis=-1, keepdims=True)
    attended = (num[...] / total).astype(jnp.bfloat16)

    load_wo.wait()
    for stage in (0, 1):
        zz = 1 - z if stage == 0 else z
        for row in range(RING):
            low = pl.multiple_of((zz * 16 + row * RING) * HD, RING * HD)
            product = dot(attended, wov[:, pl.ds(low, RING * HD)]).astype(jnp.bfloat16)
            for col in range(RING):
                tile = product[:, col * HD : (col + 1) * HD]
                s1[0, stage, row, col] = tile[:HALF]
                s1[1, stage, col, row] = tile[HALF:]

    def rs1(stage, eta, step):
        a, b = (y, x) if eta == 0 else (x, y)
        k = (stage * 2 + eta) * 3 + step - 1
        to = turn(a, step)
        return remote(
            s1.at[eta, stage, to], r1.at[eta, stage, step - 1], rs1_send.at[k], rs1_recv.at[k],
            head=head_at(z, eta, to, b, eta == 0),
        )

    def rs2(stage, eta, step):
        a, b = (y, x) if eta == 0 else (x, y)
        k = (stage * 2 + eta) * 3 + step - 1
        to = turn(b, step)
        return remote(
            s2.at[eta, stage, to], r2.at[eta, stage, step - 1], rs2_send.at[k], rs2_recv.at[k],
            head=head_at(z, eta, a, to, eta == 0),
        )

    def rs3(eta):
        return remote(s3.at[eta], r3.at[eta], rs3_send.at[eta], rs3_recv.at[eta], head=z_partner)

    for stage in (0, 1):
        for step in (2, 1, 3):
            for eta in (0, 1):
                one = rs1(stage, eta, step)
                one.start()
                sent.append(one)

    f32 = jnp.float32

    def reduce_first(stage):
        for step in (1, 3, 2):
            for eta in (0, 1):
                rs1(stage, eta, step).wait_recv()
        for eta in (0, 1):
            a = y if eta == 0 else x
            for b in range(RING):
                value = s1[eta, stage, a, b].astype(f32)
                for k in range(3):
                    value = value + r1[eta, stage, k, b].astype(f32)
                s2[eta, stage, b] = value.astype(jnp.bfloat16)
        for step in (2, 1, 3):
            for eta in (0, 1):
                one = rs2(stage, eta, step)
                one.start()
                sent.append(one)

    def reduce_second(stage, eta):
        a, b = (y, x) if eta == 0 else (x, y)
        value = s1[eta, stage, a, b].astype(f32)
        for k in range(3):
            value = value + r1[eta, stage, k, b].astype(f32)
        for step in (1, 3, 2):
            rs2(stage, eta, step).wait_recv()
        for k in range(3):
            value = value + r2[eta, stage, k].astype(f32)
        return value

    reduce_first(0)
    for eta in (0, 1):
        s3[eta] = reduce_second(0, eta).astype(jnp.bfloat16)
    for eta in (0, 1):
        one = rs3(eta)
        one.start()
        sent.append(one)
    reduce_first(1)
    for eta in (0, 1):
        t1[eta] = reduce_second(1, eta)
    for eta in (0, 1):
        rs3(eta).wait_recv()
        out_ref[pl.ds(eta * HALF, HALF), :] = (t1[eta] + r3[eta].astype(f32)).astype(jnp.bfloat16)

    for one in sent:
        one.wait_send()

    @pl.when(zl < chips - 1)
    def _():
        for one in up(ctx):
            one.wait_send()

    @pl.when(core == 0)
    def _():
        for one in over(ctx):
            one.wait_send()

    def drain(s, carry):
        slot = 2 * (zl - 1 - s) + core

        @pl.when(zl < chips - 1)
        def _():
            for one in up(slot):
                one.wait_send()

        for one in over(slot):
            one.wait_send()
        return carry

    lax.fori_loop(0, zl, drain, 0)


def shards(tokens, qkv_weight, out_weight, signs, rows):
    width = qkv_weight.shape[0]
    parts = lax.axis_size("ctx")
    flat_weight = qkv_weight.reshape(width, 3 * HD)
    sketch = sketch_matrix(signs, rows)[0]
    sketch = jnp.concatenate([sketch, sketch], axis=-1)
    bf16, f32 = jnp.bfloat16, jnp.float32
    anywhere = pl.BlockSpec(memory_space=pl.ANY)
    vmem = pl.BlockSpec(memory_space=pltpu.VMEM)
    dma = pltpu.SemaphoreType.DMA
    return pl.pallas_call(
        kernel,
        out_shape=jax.ShapeDtypeStruct((BLOCK, HD), bf16),
        in_specs=[anywhere, anywhere, anywhere, vmem],
        out_specs=vmem,
        scratch_shapes=[
            pltpu.VMEM((BLOCK, width), bf16),
            pltpu.VMEM((width, 3 * HD), bf16),
            pltpu.VMEM((HD, width), bf16),
            pltpu.VMEM((BLOCK, 3 * HD), f32),
            pltpu.VMEM((parts, BLOCK, HD), bf16),
            pltpu.VMEM((parts, HALF, HD), bf16),
            pltpu.VMEM((2, BLOCK, HD), bf16),
            pltpu.VMEM((BLOCK, HD), f32),
            pltpu.VMEM((BLOCK, HD), f32),
            pltpu.VMEM((2, 2, RING, RING, HALF, HD), bf16),
            pltpu.VMEM((2, 2, 3, RING, HALF, HD), bf16),
            pltpu.VMEM((2, 2, RING, HALF, HD), bf16),
            pltpu.VMEM((2, 2, 3, HALF, HD), bf16),
            pltpu.VMEM((2, HALF, HD), bf16),
            pltpu.VMEM((2, HALF, HD), bf16),
            pltpu.VMEM((2, HALF, HD), f32),
            dma((3,)),
            dma,
            dma,
            dma((80,)),
            dma((80,)),
            dma((2 * parts,)),
            dma((2 * parts,)),
            dma((2 * parts,)),
            dma((12,)),
            dma((12,)),
            dma((12,)),
            dma((12,)),
            dma((2,)),
            dma((2,)),
        ],
        compiler_params=pltpu.CompilerParams(collective_id=0, has_side_effects=True),
    )(tokens, flat_weight, out_weight, sketch)


def solution(mesh):
    in_specs = (
        P("ctx", "head"),
        P(None, None, "head"),
        P("head", None),
        P("head", None, None),
        P("head", None, None),
    )
    out_specs = P("ctx", "head")
    return jax.shard_map(shards, mesh=mesh, in_specs=in_specs, out_specs=out_specs, check_vma=False)
```

```python
import math

import jax
import jax.numpy as jnp
from jax import lax
from jax.experimental import pallas as pl
from jax.experimental.pallas import tpu as pltpu
from jax.sharding import PartitionSpec as P

MESH = pl.DeviceIdType.MESH
BLOCK = 256
HALF = 128
QUARTER = 64
HD = 128
RING = 4
SHIFTS = (0, 3, 1, 2)

score_scale = 2.0


def dot(left, right):
    return jnp.dot(left, right, preferred_element_type=jnp.float32)


def dot_t(left, right):
    return lax.dot_general(left, right, (((1,), (1,)), ((), ())), preferred_element_type=jnp.float32)


def turn(place, step):
    return lax.rem(place + step, RING)


def kernel(
    x_ref, w_ref, wo_ref, signs_ref, rows_ref, out_ref,
    xbuf, wv, wov, acc, kvb, sk, qf, num, wsum,
    s1, ra, r1, s2, r2, s3, r3, t1,
    load_sem, z_send, z_recv, ag_send, ag_recv,
    kv_send, kv_pass, kv_recv, rsa_send, rsa_recv, rs1_send, rs1_recv, rs2_send, rs2_recv, rs3_send, rs3_recv,
):
    head = lax.axis_index("head")
    ctx = lax.axis_index("ctx")
    chips = lax.axis_size("ctx") // 2
    z = lax.div(head, RING * RING)
    y = lax.rem(lax.div(head, RING), RING)
    x = lax.rem(head, RING)
    zl = lax.div(ctx, 2)
    core = lax.rem(ctx, 2)
    other_core = ctx + 1 - 2 * core
    z_partner = (1 - z) * RING * RING + y * RING + x
    sent = []

    def remote(src, dst, send_sem, recv_sem, **device):
        return pltpu.make_async_remote_copy(
            src_ref=src, dst_ref=dst, send_sem=send_sem, recv_sem=recv_sem,
            device_id=device, device_id_type=MESH,
        )

    def head_at(zz, eta, a, b, first_is_y):
        if first_is_y:
            return zz * RING * RING + a * RING + b
        return zz * RING * RING + b * RING + a

    own_block = xbuf.at[:, pl.ds(pl.multiple_of(head * HD, HD), HD)]
    load_x = pltpu.make_async_copy(x_ref, own_block, load_sem.at[0])
    load_w = [
        pltpu.make_async_copy(w_ref.at[j], wv.at[:, pl.ds(j * HD, HD)], load_sem.at[2 + j])
        for j in range(3)
    ]
    load_wo = pltpu.make_async_copy(wo_ref, wov, load_sem.at[1])
    load_x.start()
    for one in load_w:
        one.start()
    load_wo.start()
    barrier = pltpu.get_barrier_semaphore()
    for step in (1, 2, 3):
        for place in (z * 16 + y * RING + turn(x, step), z * 16 + turn(y, step) * RING + x):
            pl.semaphore_signal(barrier, inc=1, device_id={"head": place}, device_id_type=MESH)
    pl.semaphore_signal(barrier, inc=1, device_id={"head": z_partner}, device_id_type=MESH)
    pl.semaphore_signal(barrier, inc=1, device_id={"ctx": other_core}, device_id_type=MESH)

    @pl.when(zl > 0)
    def _():
        pl.semaphore_signal(barrier, inc=1, device_id={"ctx": ctx - 2}, device_id_type=MESH)

    @pl.when(zl < chips - 1)
    def _():
        pl.semaphore_signal(barrier, inc=1, device_id={"ctx": ctx + 2}, device_id_type=MESH)

    acc[...] = jnp.zeros_like(acc)

    signed = (2 * signs_ref[0] - 1).astype(jnp.float32)
    sampled = jnp.concatenate([rows_ref[0], rows_ref[0]], axis=1)
    entry = lax.broadcasted_iota(jnp.int32, (HD, HD), 0)
    for i in (0, 1):
        common = jnp.bitwise_and(entry, sampled[i : i + 1, :])
        for shift in (4, 2, 1):
            common = jnp.bitwise_xor(common, jnp.right_shift(common, shift))
        parity = jnp.bitwise_and(common, 1)
        sk[i] = (1 - 2 * parity).astype(jnp.float32).astype(jnp.bfloat16)

    pl.semaphore_wait(barrier, 8 + lax.min(zl, 1) + lax.min(chips - 1 - zl, 1))

    load_x.wait()

    z_copy = remote(own_block, own_block, z_send, z_recv, head=z_partner)
    z_copy.start()
    sent.append(z_copy)

    def line(stage, eta, phase, shift):
        first_is_y = eta == 1
        a, b = (y, x) if first_is_y else (x, y)
        zz = z if stage == 0 else 1 - z
        base = (stage * 2 + eta) * 20 + (0 if phase == 0 else 4 + 4 * shift)
        pos = a if phase == 0 else b

        def device(place):
            return head_at(z, eta, place, b, first_is_y) if phase == 0 else head_at(z, eta, a, place, first_is_y)

        def piece(place, low, count):
            if phase == 0:
                t = head_at(zz, eta, place, b, first_is_y)
            else:
                t = head_at(zz, eta, turn(a, SHIFTS[shift]), place, first_is_y)
            return xbuf.at[pl.ds(eta * HALF + low, count), pl.ds(pl.multiple_of(t * HD, HD), HD)]

        def copy(k, what, step):
            return remote(what, what, ag_send.at[base + k], ag_recv.at[base + k], head=device(turn(pos, step)))

        def send(k, what, step):
            one = copy(k, what, step)
            one.start()
            sent.append(one)

        def start():
            send(0, piece(pos, 0, HALF), 1)
            send(1, piece(pos, 0, HALF), 3)

        def relay(side):
            if side == 0:
                copy(0, piece(turn(pos, 3), 0, HALF), 1).wait_recv()
                send(2, piece(turn(pos, 3), 0, QUARTER), 1)
            else:
                copy(1, piece(turn(pos, 1), 0, HALF), 3).wait_recv()
                send(3, piece(turn(pos, 1), QUARTER, QUARTER), 3)

        def finish():
            copy(2, piece(turn(pos, 2), 0, QUARTER), 1).wait_recv()
            copy(3, piece(turn(pos, 2), QUARTER, QUARTER), 3).wait_recv()

        return start, relay, finish

    def spread(stage, filler):
        first = [line(stage, eta, 0, 0) for eta in (0, 1)]
        second = [[line(stage, eta, 1, shift) for shift in range(4)] for eta in (0, 1)]
        for eta in (0, 1):
            first[eta][0]()
        for eta in (0, 1):
            second[eta][0][0]()
        filler()
        for side in (0, 1):
            for eta in (0, 1):
                first[eta][1](side)
                second[eta][1 + side][0]()
        for eta in (0, 1):
            for side in (0, 1):
                second[eta][0][1](side)
        for eta in (0, 1):
            first[eta][2]()
            second[eta][3][0]()
        for shift in (1, 2, 3):
            for side in (0, 1):
                for eta in (0, 1):
                    second[eta][shift][1](side)
        for shift in range(4):
            for eta in (0, 1):
                second[eta][shift][2]()

    chunk = 4 * HD

    def project(zz):
        def one(k, carry):
            low = pl.multiple_of(zz * (16 * HD) + k * chunk, chunk)
            acc[...] += dot(xbuf[:, pl.ds(low, chunk)], wv[pl.ds(low, chunk), :])
            return carry

        lax.fori_loop(0, 4, one, 0)

    spread(0, lambda: None)
    for one in load_w:
        one.wait()
    z_block = xbuf.at[:, pl.ds(pl.multiple_of(z_partner * HD, HD), HD)]
    remote(z_block, z_block, z_send, z_recv, head=z_partner).wait_recv()
    spread(1, lambda: project(z))
    project(1 - z)

    def normalize(raw):
        return (raw * lax.rsqrt(jnp.mean(raw * raw, axis=-1, keepdims=True) + 1e-06)).astype(jnp.bfloat16)

    factor = score_scale * score_scale / (HD * math.sqrt(QUARTER))

    def twice(normed):
        wide = normed.astype(jnp.float32)
        first = dot((wide * signed[0:1, :]).astype(jnp.bfloat16), sk[0])
        second = dot((wide * signed[1:2, :]).astype(jnp.bfloat16), sk[1])
        return factor * first * second

    kn = normalize(acc[:, HD : 2 * HD])
    kf = twice(kn)
    low_half = lax.broadcasted_iota(jnp.int32, (HALF, HD), 1) < QUARTER
    kvb[ctx, 0] = jnp.where(low_half, kf[:HALF], kf[HALF:]).astype(jnp.bfloat16)
    kvb[ctx, 1] = acc[:HALF, 2 * HD :].astype(jnp.bfloat16)
    kvb[ctx, 2] = acc[HALF:, 2 * HD :].astype(jnp.bfloat16)
    qn = normalize(acc[:, :HD])
    qd = twice(qn)
    lanes_low = lax.broadcasted_iota(jnp.int32, (BLOCK, HD), 1) < QUARTER
    qf[0] = jnp.where(lanes_low, qd, 0.0).astype(jnp.bfloat16)
    qf[1] = jnp.where(lanes_low, 0.0, qd).astype(jnp.bfloat16)

    def kv(slot, piece, sems, target):
        k = 3 * slot + piece
        return remote(kvb.at[slot, piece], kvb.at[slot, piece], sems.at[k], kv_recv.at[k], ctx=target)

    def up(slot):
        return [kv(slot, piece, kv_send, ctx + 2) for piece in range(3)]

    def over(slot):
        return [kv(slot, piece, kv_pass, other_core) for piece in range(3)]

    def values(slot):
        return kvb[slot, pl.ds(1, 2)].reshape(BLOCK, HD)

    @pl.when(zl < chips - 1)
    def _():
        for one in up(ctx):
            one.start()

    @pl.when(core == 0)
    def _():
        for one in over(ctx):
            one.start()

    scores = dot_t(qn, kn)
    causal = (
        lax.broadcasted_iota(jnp.int32, (BLOCK, BLOCK), 0)
        >= lax.broadcasted_iota(jnp.int32, (BLOCK, BLOCK), 1)
    )
    scaled = scores * (score_scale / HD)
    square = scaled * scaled
    weights = jnp.where(causal, square * square, 0.0)
    wsum[...] = weights[:, :HD] + weights[:, HD:]
    num[...] = dot(weights.astype(jnp.bfloat16), values(ctx))

    def attend(slot):
        packed = kvb[slot, 0]
        left = dot_t(qf[0], packed)
        right = dot_t(qf[1], packed)
        left = left * left
        right = right * right
        wsum[...] += left + right
        both = jnp.concatenate([left.astype(jnp.bfloat16), right.astype(jnp.bfloat16)], axis=1)
        num[...] += dot(both, values(slot))

    @pl.when(core == 1)
    def _():
        for one in over(2 * zl):
            one.wait_recv()
        attend(2 * zl)

    def earlier(s, carry):
        chip = zl - 1 - s
        slot = 2 * chip + core
        for piece in range(3):
            kv(slot, piece, kv_send, other_core).wait_recv()

            @pl.when(zl < chips - 1)
            def _():
                kv(slot, piece, kv_send, ctx + 2).start()

            kv(slot, piece, kv_pass, other_core).start()

        attend(slot)
        second = 2 * chip + 1 - core
        for one in over(second):
            one.wait_recv()
        attend(second)
        return carry

    lax.fori_loop(0, zl, earlier, 0)

    total = 1.0 + jnp.sum(wsum[...], axis=-1, keepdims=True)
    attended = (num[...] / total).astype(jnp.bfloat16)

    load_wo.wait()
    for stage in (0, 1):
        zz = 1 - z if stage == 0 else z
        for row in range(RING):
            low = pl.multiple_of((zz * 16 + row * RING) * HD, RING * HD)
            product = dot(attended, wov[:, pl.ds(low, RING * HD)]).astype(jnp.bfloat16)
            for col in range(RING):
                tile = product[:, col * HD : (col + 1) * HD]
                s1[0, stage, row, col] = tile[:HALF]
                s1[1, stage, col, row] = tile[HALF:]

    PAIR = RING // 2

    def ring(eta, step):
        a, b = (y, x) if eta == 0 else (x, y)
        to = turn(a, step)
        return to, head_at(z, eta, to, b, eta == 0)

    def rsa(stage, eta, side):
        k = (stage * 2 + eta) * 2 + side
        far, _ = ring(eta, 2)
        _, device = ring(eta, 1 if side == 0 else 3)
        return remote(
            s1.at[eta, stage, far, pl.ds(side * PAIR, PAIR)], ra.at[eta, stage, side],
            rsa_send.at[k], rsa_recv.at[k], head=device,
        )

    def rs1(stage, eta, side, half):
        k = ((stage * 2 + eta) * 2 + side) * 2 + half
        to, device = ring(eta, 1 if side == 0 else 3)
        return remote(
            s1.at[eta, stage, to, pl.ds(half * PAIR, PAIR)], r1.at[eta, stage, side, pl.ds(half * PAIR, PAIR)],
            rs1_send.at[k], rs1_recv.at[k], head=device,
        )

    def rs2(stage, eta, step):
        a, b = (y, x) if eta == 0 else (x, y)
        k = (stage * 2 + eta) * 3 + step - 1
        to = turn(b, step)
        return remote(
            s2.at[eta, stage, to], r2.at[eta, stage, step - 1], rs2_send.at[k], rs2_recv.at[k],
            head=head_at(z, eta, a, to, eta == 0),
        )

    def rs3(eta):
        return remote(s3.at[eta], r3.at[eta], rs3_send.at[eta], rs3_recv.at[eta], head=z_partner)

    def begin(one):
        one.start()
        sent.append(one)

    ways = [(eta, side) for eta in (0, 1) for side in (0, 1)]
    for stage in (0, 1):
        for eta, side in ways:
            begin(rsa(stage, eta, side))
        for eta, side in ways:
            begin(rs1(stage, eta, side, 1 - side))

    f32 = jnp.float32

    def relay_first(stage):
        for eta, side in ways:
            rsa(stage, eta, side).wait_recv()
            to, _ = ring(eta, 1 if side == 0 else 3)
            part = pl.ds(side * PAIR, PAIR)
            s1[eta, stage, to, part] = (
                s1[eta, stage, to, part].astype(f32) + ra[eta, stage, side].astype(f32)
            ).astype(jnp.bfloat16)
        for eta, side in ways:
            begin(rs1(stage, eta, side, side))

    def reduce_first(stage):
        for eta, side in ways:
            rs1(stage, eta, side, 1 - side).wait_recv()
        for eta, side in ways:
            rs1(stage, eta, side, side).wait_recv()
        for eta in (0, 1):
            a = y if eta == 0 else x
            for b in range(RING):
                value = s1[eta, stage, a, b].astype(f32)
                for k in range(2):
                    value = value + r1[eta, stage, k, b].astype(f32)
                s2[eta, stage, b] = value.astype(jnp.bfloat16)
        for step in (2, 1, 3):
            for eta in (0, 1):
                one = rs2(stage, eta, step)
                one.start()
                sent.append(one)

    def reduce_second(stage, eta):
        a, b = (y, x) if eta == 0 else (x, y)
        value = s1[eta, stage, a, b].astype(f32)
        for k in range(2):
            value = value + r1[eta, stage, k, b].astype(f32)
        for step in (1, 3, 2):
            rs2(stage, eta, step).wait_recv()
        for k in range(3):
            value = value + r2[eta, stage, k].astype(f32)
        return value

    relay_first(0)
    relay_first(1)
    reduce_first(0)
    for eta in (0, 1):
        s3[eta] = reduce_second(0, eta).astype(jnp.bfloat16)
    for eta in (0, 1):
        one = rs3(eta)
        one.start()
        sent.append(one)
    reduce_first(1)
    for eta in (0, 1):
        t1[eta] = reduce_second(1, eta)
    for eta in (0, 1):
        rs3(eta).wait_recv()
        out_ref[pl.ds(eta * HALF, HALF), :] = (t1[eta] + r3[eta].astype(f32)).astype(jnp.bfloat16)

    for one in sent:
        one.wait_send()

    @pl.when(zl < chips - 1)
    def _():
        for one in up(ctx):
            one.wait_send()

    @pl.when(core == 0)
    def _():
        for one in over(ctx):
            one.wait_send()

    def drain(s, carry):
        slot = 2 * (zl - 1 - s) + core

        @pl.when(zl < chips - 1)
        def _():
            for one in up(slot):
                one.wait_send()

        for one in over(slot):
            one.wait_send()
        return carry

    lax.fori_loop(0, zl, drain, 0)


def shards(tokens, qkv_weight, out_weight, signs, rows):
    width = qkv_weight.shape[0]
    parts = lax.axis_size("ctx")
    by_kind = qkv_weight.transpose(1, 0, 2)
    bf16, f32 = jnp.bfloat16, jnp.float32
    anywhere = pl.BlockSpec(memory_space=pl.ANY)
    vmem = pl.BlockSpec(memory_space=pltpu.VMEM)
    dma = pltpu.SemaphoreType.DMA
    return pl.pallas_call(
        kernel,
        out_shape=jax.ShapeDtypeStruct((BLOCK, HD), bf16),
        in_specs=[anywhere, anywhere, anywhere, vmem, vmem],
        out_specs=vmem,
        scratch_shapes=[
            pltpu.VMEM((BLOCK, width), bf16),
            pltpu.VMEM((width, 3 * HD), bf16),
            pltpu.VMEM((HD, width), bf16),
            pltpu.VMEM((BLOCK, 3 * HD), f32),
            pltpu.VMEM((parts, 3, HALF, HD), bf16),
            pltpu.VMEM((2, HD, HD), bf16),
            pltpu.VMEM((2, BLOCK, HD), bf16),
            pltpu.VMEM((BLOCK, HD), f32),
            pltpu.VMEM((BLOCK, HD), f32),
            pltpu.VMEM((2, 2, RING, RING, HALF, HD), bf16),
            pltpu.VMEM((2, 2, 2, RING // 2, HALF, HD), bf16),
            pltpu.VMEM((2, 2, 2, RING, HALF, HD), bf16),
            pltpu.VMEM((2, 2, RING, HALF, HD), bf16),
            pltpu.VMEM((2, 2, 3, HALF, HD), bf16),
            pltpu.VMEM((2, HALF, HD), bf16),
            pltpu.VMEM((2, HALF, HD), bf16),
            pltpu.VMEM((2, HALF, HD), f32),
            dma((5,)),
            dma,
            dma,
            dma((80,)),
            dma((80,)),
            dma((3 * parts,)),
            dma((3 * parts,)),
            dma((3 * parts,)),
            dma((8,)),
            dma((8,)),
            dma((16,)),
            dma((16,)),
            dma((12,)),
            dma((12,)),
            dma((2,)),
            dma((2,)),
        ],
        compiler_params=pltpu.CompilerParams(collective_id=0, has_side_effects=True),
    )(tokens, by_kind, out_weight, signs, rows)


def solution(mesh):
    in_specs = (
        P("ctx", "head"),
        P(None, None, "head"),
        P("head", None),
        P("head", None, None),
        P("head", None, None),
    )
    out_specs = P("ctx", "head")
    return jax.shard_map(shards, mesh=mesh, in_specs=in_specs, out_specs=out_specs, check_vma=False)
```

```python
import math

import jax
import jax.numpy as jnp
from jax import lax
from jax.experimental import pallas as pl
from jax.experimental.pallas import tpu as pltpu
from jax.sharding import PartitionSpec as P

MESH = pl.DeviceIdType.MESH
BLOCK = 256
HALF = 128
QUARTER = 64
HD = 128
RING = 4
SHIFTS = (0, 3, 1, 2)

score_scale = 2.0


def dot(left, right):
    return jnp.dot(left, right, preferred_element_type=jnp.float32)


def dot_t(left, right):
    return lax.dot_general(left, right, (((1,), (1,)), ((), ())), preferred_element_type=jnp.float32)


def turn(place, step):
    return lax.rem(place + step, RING)


def kernel(
    x_ref, w_ref, wo_ref, signs_ref, rows_ref, out_ref,
    xbuf, wv, wov, acc, kvb, sk, qf, num, wsum,
    s1, ra, r1, s2, r2, s3, r3, t1,
    load_sem, z_send, z_recv, ag_send, ag_recv,
    kv_send, kv_pass, kv_recv, rsa_send, rsa_recv, rs1_send, rs1_recv, rs2_send, rs2_recv, rs3_send, rs3_recv,
):
    head = lax.axis_index("head")
    ctx = lax.axis_index("ctx")
    chips = lax.axis_size("ctx") // 2
    z = lax.div(head, RING * RING)
    y = lax.rem(lax.div(head, RING), RING)
    x = lax.rem(head, RING)
    zl = lax.div(ctx, 2)
    core = lax.rem(ctx, 2)
    other_core = ctx + 1 - 2 * core
    z_partner = (1 - z) * RING * RING + y * RING + x
    sent = []

    def remote(src, dst, send_sem, recv_sem, **device):
        return pltpu.make_async_remote_copy(
            src_ref=src, dst_ref=dst, send_sem=send_sem, recv_sem=recv_sem,
            device_id=device, device_id_type=MESH,
        )

    def head_at(zz, eta, a, b, first_is_y):
        if first_is_y:
            return zz * RING * RING + a * RING + b
        return zz * RING * RING + b * RING + a

    own_block = xbuf.at[head]
    load_x = pltpu.make_async_copy(x_ref, own_block, load_sem.at[0])
    load_w = [
        pltpu.make_async_copy(w_ref.at[j], wv.at[:, pl.ds(j * HD, HD)], load_sem.at[2 + j])
        for j in range(3)
    ]
    load_wo = pltpu.make_async_copy(wo_ref, wov, load_sem.at[1])
    load_x.start()
    for one in load_w:
        one.start()
    load_wo.start()
    barrier = pltpu.get_barrier_semaphore()
    for step in (1, 2, 3):
        for place in (z * 16 + y * RING + turn(x, step), z * 16 + turn(y, step) * RING + x):
            pl.semaphore_signal(barrier, inc=1, device_id={"head": place}, device_id_type=MESH)
    pl.semaphore_signal(barrier, inc=1, device_id={"head": z_partner}, device_id_type=MESH)
    pl.semaphore_signal(barrier, inc=1, device_id={"ctx": other_core}, device_id_type=MESH)

    @pl.when(zl > 0)
    def _():
        pl.semaphore_signal(barrier, inc=1, device_id={"ctx": ctx - 2}, device_id_type=MESH)

    @pl.when(zl < chips - 1)
    def _():
        pl.semaphore_signal(barrier, inc=1, device_id={"ctx": ctx + 2}, device_id_type=MESH)

    acc[...] = jnp.zeros_like(acc)

    signed = (2 * signs_ref[0] - 1).astype(jnp.float32)
    sampled = jnp.concatenate([rows_ref[0], rows_ref[0]], axis=1)
    entry = lax.broadcasted_iota(jnp.int32, (HD, HD), 0)
    for i in (0, 1):
        common = jnp.bitwise_and(entry, sampled[i : i + 1, :])
        for shift in (4, 2, 1):
            common = jnp.bitwise_xor(common, jnp.right_shift(common, shift))
        parity = jnp.bitwise_and(common, 1)
        sk[i] = (1 - 2 * parity).astype(jnp.float32).astype(jnp.bfloat16)

    pl.semaphore_wait(barrier, 8 + lax.min(zl, 1) + lax.min(chips - 1 - zl, 1))

    load_x.wait()

    z_copy = remote(own_block, own_block, z_send, z_recv, head=z_partner)
    z_copy.start()
    sent.append(z_copy)

    def line(stage, eta, phase, shift):
        first_is_y = eta == 1
        a, b = (y, x) if first_is_y else (x, y)
        zz = z if stage == 0 else 1 - z
        base = (stage * 2 + eta) * 20 + (0 if phase == 0 else 4 + 4 * shift)
        pos = a if phase == 0 else b

        def device(place):
            return head_at(z, eta, place, b, first_is_y) if phase == 0 else head_at(z, eta, a, place, first_is_y)

        def piece(place, low, count):
            if phase == 0:
                t = head_at(zz, eta, place, b, first_is_y)
            else:
                t = head_at(zz, eta, turn(a, SHIFTS[shift]), place, first_is_y)
            return xbuf.at[t, eta, pl.ds(low, count)]

        def copy(k, what, step):
            return remote(what, what, ag_send.at[base + k], ag_recv.at[base + k], head=device(turn(pos, step)))

        def send(k, what, step):
            one = copy(k, what, step)
            one.start()
            sent.append(one)

        def start():
            send(0, piece(pos, 0, HALF), 1)
            send(1, piece(pos, 0, HALF), 3)

        def relay(side):
            if side == 0:
                copy(0, piece(turn(pos, 3), 0, HALF), 1).wait_recv()
                send(2, piece(turn(pos, 3), 0, QUARTER), 1)
            else:
                copy(1, piece(turn(pos, 1), 0, HALF), 3).wait_recv()
                send(3, piece(turn(pos, 1), QUARTER, QUARTER), 3)

        def finish():
            copy(2, piece(turn(pos, 2), 0, QUARTER), 1).wait_recv()
            copy(3, piece(turn(pos, 2), QUARTER, QUARTER), 3).wait_recv()

        return start, relay, finish

    def spread(stage, fillers):
        first = [line(stage, eta, 0, 0) for eta in (0, 1)]
        second = [[line(stage, eta, 1, shift) for shift in range(4)] for eta in (0, 1)]
        for eta in (0, 1):
            first[eta][0]()
        for eta in (0, 1):
            second[eta][0][0]()
        fillers[0]()
        for side in (0, 1):
            for eta in (0, 1):
                first[eta][1](side)
                second[eta][1 + side][0]()
        fillers[1]()
        for eta in (0, 1):
            for side in (0, 1):
                second[eta][0][1](side)
        fillers[2]()
        for eta in (0, 1):
            first[eta][2]()
            second[eta][3][0]()
        fillers[3]()
        for shift in (1, 2, 3):
            for side in (0, 1):
                for eta in (0, 1):
                    second[eta][shift][1](side)
            fillers[3 + shift]()

        def finish():
            for shift in range(4):
                for eta in (0, 1):
                    second[eta][shift][2]()

        return finish

    def project(zz, k):
        t = zz * 16 + k * RING
        part = jnp.concatenate([xbuf[t + j].reshape(BLOCK, HD) for j in range(RING)], axis=1)
        acc[...] += dot(part, wv[pl.ds(pl.multiple_of(t * HD, RING * HD), RING * HD), :])

    def idle():
        pass

    finish_own = spread(0, [idle] * 7)
    for one in load_w:
        one.wait()
    z_block = xbuf.at[z_partner]
    remote(z_block, z_block, z_send, z_recv, head=z_partner).wait_recv()
    steps = [lambda k=k: project(z, k) for k in range(RING)]
    finish_other = spread(1, [finish_own, steps[0], steps[1], steps[2], steps[3], idle, idle])
    finish_other()
    for k in range(RING):
        project(1 - z, k)

    def normalize(raw):
        return (raw * lax.rsqrt(jnp.mean(raw * raw, axis=-1, keepdims=True) + 1e-06)).astype(jnp.bfloat16)

    factor = score_scale * score_scale / (HD * math.sqrt(QUARTER))

    def twice(normed):
        wide = normed.astype(jnp.float32)
        first = dot((wide * signed[0:1, :]).astype(jnp.bfloat16), sk[0])
        second = dot((wide * signed[1:2, :]).astype(jnp.bfloat16), sk[1])
        return factor * first * second

    kn = normalize(acc[:, HD : 2 * HD])
    kf = twice(kn)
    low_half = lax.broadcasted_iota(jnp.int32, (HALF, HD), 1) < QUARTER
    kvb[ctx, 0] = jnp.where(low_half, kf[:HALF], kf[HALF:]).astype(jnp.bfloat16)
    kvb[ctx, 1] = acc[:HALF, 2 * HD :].astype(jnp.bfloat16)
    kvb[ctx, 2] = acc[HALF:, 2 * HD :].astype(jnp.bfloat16)
    qn = normalize(acc[:, :HD])
    qd = twice(qn)
    lanes_low = lax.broadcasted_iota(jnp.int32, (BLOCK, HD), 1) < QUARTER
    qf[0] = jnp.where(lanes_low, qd, 0.0).astype(jnp.bfloat16)
    qf[1] = jnp.where(lanes_low, 0.0, qd).astype(jnp.bfloat16)

    def kv(slot, piece, sems, target):
        k = 3 * slot + piece
        return remote(kvb.at[slot, piece], kvb.at[slot, piece], sems.at[k], kv_recv.at[k], ctx=target)

    def up(slot):
        return [kv(slot, piece, kv_send, ctx + 2) for piece in range(3)]

    def over(slot):
        return [kv(slot, piece, kv_pass, other_core) for piece in range(3)]

    def values(slot):
        return kvb[slot, pl.ds(1, 2)].reshape(BLOCK, HD)

    @pl.when(zl < chips - 1)
    def _():
        for one in up(ctx):
            one.start()

    @pl.when(core == 0)
    def _():
        for one in over(ctx):
            one.start()

    scores = dot_t(qn, kn)
    causal = (
        lax.broadcasted_iota(jnp.int32, (BLOCK, BLOCK), 0)
        >= lax.broadcasted_iota(jnp.int32, (BLOCK, BLOCK), 1)
    )
    scaled = scores * (score_scale / HD)
    square = scaled * scaled
    weights = jnp.where(causal, square * square, 0.0)
    wsum[...] = weights[:, :HD] + weights[:, HD:]
    num[...] = dot(weights.astype(jnp.bfloat16), values(ctx))

    def attend(slot):
        packed = kvb[slot, 0]
        left = dot_t(qf[0], packed)
        right = dot_t(qf[1], packed)
        left = left * left
        right = right * right
        wsum[...] += left + right
        both = jnp.concatenate([left.astype(jnp.bfloat16), right.astype(jnp.bfloat16)], axis=1)
        num[...] += dot(both, values(slot))

    @pl.when(core == 1)
    def _():
        for one in over(2 * zl):
            one.wait_recv()
        attend(2 * zl)

    def earlier(s, carry):
        chip = zl - 1 - s
        slot = 2 * chip + core
        for piece in range(3):
            kv(slot, piece, kv_send, other_core).wait_recv()

            @pl.when(zl < chips - 1)
            def _():
                kv(slot, piece, kv_send, ctx + 2).start()

            kv(slot, piece, kv_pass, other_core).start()

        attend(slot)
        second = 2 * chip + 1 - core
        for one in over(second):
            one.wait_recv()
        attend(second)
        return carry

    lax.fori_loop(0, zl, earlier, 0)

    total = 1.0 + jnp.sum(wsum[...], axis=-1, keepdims=True)
    attended = (num[...] / total).astype(jnp.bfloat16)

    load_wo.wait()
    for stage in (0, 1):
        zz = 1 - z if stage == 0 else z
        for row in range(RING):
            low = pl.multiple_of((zz * 16 + row * RING) * HD, RING * HD)
            product = dot(attended, wov[:, pl.ds(low, RING * HD)]).astype(jnp.bfloat16)
            for col in range(RING):
                tile = product[:, col * HD : (col + 1) * HD]
                s1[0, stage, row, col] = tile[:HALF]
                s1[1, stage, col, row] = tile[HALF:]

    PAIR = RING // 2

    def ring(eta, step):
        a, b = (y, x) if eta == 0 else (x, y)
        to = turn(a, step)
        return to, head_at(z, eta, to, b, eta == 0)

    def rsa(stage, eta, side):
        k = (stage * 2 + eta) * 2 + side
        far, _ = ring(eta, 2)
        _, device = ring(eta, 1 if side == 0 else 3)
        return remote(
            s1.at[eta, stage, far, pl.ds(side * PAIR, PAIR)], ra.at[eta, stage, side],
            rsa_send.at[k], rsa_recv.at[k], head=device,
        )

    def rs1(stage, eta, side, half):
        k = ((stage * 2 + eta) * 2 + side) * 2 + half
        to, device = ring(eta, 1 if side == 0 else 3)
        return remote(
            s1.at[eta, stage, to, pl.ds(half * PAIR, PAIR)], r1.at[eta, stage, side, pl.ds(half * PAIR, PAIR)],
            rs1_send.at[k], rs1_recv.at[k], head=device,
        )

    def rs2(stage, eta, step):
        a, b = (y, x) if eta == 0 else (x, y)
        k = (stage * 2 + eta) * 3 + step - 1
        to = turn(b, step)
        return remote(
            s2.at[eta, stage, to], r2.at[eta, stage, step - 1], rs2_send.at[k], rs2_recv.at[k],
            head=head_at(z, eta, a, to, eta == 0),
        )

    def rs3(eta):
        return remote(s3.at[eta], r3.at[eta], rs3_send.at[eta], rs3_recv.at[eta], head=z_partner)

    def begin(one):
        one.start()
        sent.append(one)

    ways = [(eta, side) for eta in (0, 1) for side in (0, 1)]
    for stage in (0, 1):
        for eta, side in ways:
            begin(rsa(stage, eta, side))
        for eta, side in ways:
            begin(rs1(stage, eta, side, 1 - side))

    f32 = jnp.float32

    def relay_first(stage):
        for eta, side in ways:
            rsa(stage, eta, side).wait_recv()
            to, _ = ring(eta, 1 if side == 0 else 3)
            part = pl.ds(side * PAIR, PAIR)
            s1[eta, stage, to, part] = (
                s1[eta, stage, to, part].astype(f32) + ra[eta, stage, side].astype(f32)
            ).astype(jnp.bfloat16)
        for eta, side in ways:
            begin(rs1(stage, eta, side, side))

    def reduce_first(stage):
        for eta, side in ways:
            rs1(stage, eta, side, 1 - side).wait_recv()
        for eta, side in ways:
            rs1(stage, eta, side, side).wait_recv()
        for eta in (0, 1):
            a = y if eta == 0 else x
            for b in range(RING):
                value = s1[eta, stage, a, b].astype(f32)
                for k in range(2):
                    value = value + r1[eta, stage, k, b].astype(f32)
                s2[eta, stage, b] = value.astype(jnp.bfloat16)
        for step in (2, 1, 3):
            for eta in (0, 1):
                one = rs2(stage, eta, step)
                one.start()
                sent.append(one)

    def reduce_second(stage, eta):
        a, b = (y, x) if eta == 0 else (x, y)
        value = s1[eta, stage, a, b].astype(f32)
        for k in range(2):
            value = value + r1[eta, stage, k, b].astype(f32)
        for step in (1, 3, 2):
            rs2(stage, eta, step).wait_recv()
        for k in range(3):
            value = value + r2[eta, stage, k].astype(f32)
        return value

    relay_first(0)
    relay_first(1)
    reduce_first(0)
    for eta in (0, 1):
        s3[eta] = reduce_second(0, eta).astype(jnp.bfloat16)
    for eta in (0, 1):
        one = rs3(eta)
        one.start()
        sent.append(one)
    reduce_first(1)
    for eta in (0, 1):
        t1[eta] = reduce_second(1, eta)
    for eta in (0, 1):
        rs3(eta).wait_recv()
        out_ref[pl.ds(eta * HALF, HALF), :] = (t1[eta] + r3[eta].astype(f32)).astype(jnp.bfloat16)

    for one in sent:
        one.wait_send()

    @pl.when(zl < chips - 1)
    def _():
        for one in up(ctx):
            one.wait_send()

    @pl.when(core == 0)
    def _():
        for one in over(ctx):
            one.wait_send()

    def drain(s, carry):
        slot = 2 * (zl - 1 - s) + core

        @pl.when(zl < chips - 1)
        def _():
            for one in up(slot):
                one.wait_send()

        for one in over(slot):
            one.wait_send()
        return carry

    lax.fori_loop(0, zl, drain, 0)


def shards(tokens, qkv_weight, out_weight, signs, rows):
    width = qkv_weight.shape[0]
    parts = lax.axis_size("ctx")
    by_kind = qkv_weight.transpose(1, 0, 2)
    bf16, f32 = jnp.bfloat16, jnp.float32
    anywhere = pl.BlockSpec(memory_space=pl.ANY)
    vmem = pl.BlockSpec(memory_space=pltpu.VMEM)
    dma = pltpu.SemaphoreType.DMA
    return pl.pallas_call(
        kernel,
        out_shape=jax.ShapeDtypeStruct((BLOCK, HD), bf16),
        in_specs=[anywhere, anywhere, anywhere, vmem, vmem],
        out_specs=vmem,
        scratch_shapes=[
            pltpu.VMEM((width // HD, 2, HALF, HD), bf16),
            pltpu.VMEM((width, 3 * HD), bf16),
            pltpu.VMEM((HD, width), bf16),
            pltpu.VMEM((BLOCK, 3 * HD), f32),
            pltpu.VMEM((parts, 3, HALF, HD), bf16),
            pltpu.VMEM((2, HD, HD), bf16),
            pltpu.VMEM((2, BLOCK, HD), bf16),
            pltpu.VMEM((BLOCK, HD), f32),
            pltpu.VMEM((BLOCK, HD), f32),
            pltpu.VMEM((2, 2, RING, RING, HALF, HD), bf16),
            pltpu.VMEM((2, 2, 2, RING // 2, HALF, HD), bf16),
            pltpu.VMEM((2, 2, 2, RING, HALF, HD), bf16),
            pltpu.VMEM((2, 2, RING, HALF, HD), bf16),
            pltpu.VMEM((2, 2, 3, HALF, HD), bf16),
            pltpu.VMEM((2, HALF, HD), bf16),
            pltpu.VMEM((2, HALF, HD), bf16),
            pltpu.VMEM((2, HALF, HD), f32),
            dma((5,)),
            dma,
            dma,
            dma((80,)),
            dma((80,)),
            dma((3 * parts,)),
            dma((3 * parts,)),
            dma((3 * parts,)),
            dma((8,)),
            dma((8,)),
            dma((16,)),
            dma((16,)),
            dma((12,)),
            dma((12,)),
            dma((2,)),
            dma((2,)),
        ],
        compiler_params=pltpu.CompilerParams(collective_id=0, has_side_effects=True),
    )(tokens.reshape(2, HALF, HD), by_kind, out_weight, signs, rows)


def solution(mesh):
    in_specs = (
        P("ctx", "head"),
        P(None, None, "head"),
        P("head", None),
        P("head", None, None),
        P("head", None, None),
    )
    out_specs = P("ctx", "head")
    return jax.shard_map(shards, mesh=mesh, in_specs=in_specs, out_specs=out_specs, check_vma=False)
```

```python
import math

import jax
import jax.numpy as jnp
from jax import lax
from jax.experimental import pallas as pl
from jax.experimental.pallas import tpu as pltpu
from jax.sharding import PartitionSpec as P

MESH = pl.DeviceIdType.MESH
BLOCK = 256
HALF = 128
QUARTER = 64
HD = 128
NEAR = 32
VIA = 1
RING = 4
SHIFTS = (0, 3, 1, 2)

score_scale = 2.0


def dot(left, right):
    return jnp.dot(left, right, preferred_element_type=jnp.float32)


def dot_t(left, right):
    return lax.dot_general(left, right, (((1,), (1,)), ((), ())), preferred_element_type=jnp.float32)


def turn(place, step):
    return lax.rem(place + step, RING)


def kernel(
    x_ref, w_ref, wo_ref, signs_ref, rows_ref, out_ref,
    xbuf, wv, wov, acc, kvb, sk, qf, num, wsum,
    s1, ra, r1, s2, r2, s3, r3, t1,
    load_sem, z_send, z_recv, ag_send, ag_recv,
    kv_send, kv_pass, kv_recv, rsa_send, rsa_recv, rs1_send, rs1_recv, rs2_send, rs2_recv, rs3_send, rs3_recv,
):
    head = lax.axis_index("head")
    ctx = lax.axis_index("ctx")
    chips = lax.axis_size("ctx") // 2
    z = lax.div(head, RING * RING)
    y = lax.rem(lax.div(head, RING), RING)
    x = lax.rem(head, RING)
    zl = lax.div(ctx, 2)
    core = lax.rem(ctx, 2)
    other_core = ctx + 1 - 2 * core
    z_partner = (1 - z) * RING * RING + y * RING + x
    sent = []

    def remote(src, dst, send_sem, recv_sem, **device):
        return pltpu.make_async_remote_copy(
            src_ref=src, dst_ref=dst, send_sem=send_sem, recv_sem=recv_sem,
            device_id=device, device_id_type=MESH,
        )

    def head_at(zz, eta, a, b, first_is_y):
        if first_is_y:
            return zz * RING * RING + a * RING + b
        return zz * RING * RING + b * RING + a

    own_block = xbuf.at[head]
    load_x = pltpu.make_async_copy(x_ref, own_block, load_sem.at[0])
    load_w = [
        pltpu.make_async_copy(w_ref.at[j], wv.at[:, pl.ds(j * HD, HD)], load_sem.at[2 + j])
        for j in range(3)
    ]
    load_wo = pltpu.make_async_copy(wo_ref, wov, load_sem.at[1])
    load_x.start()
    for one in load_w:
        one.start()
    load_wo.start()
    barrier = pltpu.get_barrier_semaphore()
    for step in (1, 2, 3):
        for place in (z * 16 + y * RING + turn(x, step), z * 16 + turn(y, step) * RING + x):
            pl.semaphore_signal(barrier, inc=1, device_id={"head": place}, device_id_type=MESH)
    pl.semaphore_signal(barrier, inc=1, device_id={"head": z_partner}, device_id_type=MESH)
    pl.semaphore_signal(barrier, inc=1, device_id={"ctx": other_core}, device_id_type=MESH)

    @pl.when(zl > 0)
    def _():
        pl.semaphore_signal(barrier, inc=1, device_id={"ctx": ctx - 2}, device_id_type=MESH)

    @pl.when(zl < chips - 1)
    def _():
        pl.semaphore_signal(barrier, inc=1, device_id={"ctx": ctx + 2}, device_id_type=MESH)

    acc[...] = jnp.zeros_like(acc)

    signed = (2 * signs_ref[0] - 1).astype(jnp.float32)
    sampled = jnp.concatenate([rows_ref[0], rows_ref[0]], axis=1)
    entry = lax.broadcasted_iota(jnp.int32, (HD, HD), 0)
    for i in (0, 1):
        common = jnp.bitwise_and(entry, sampled[i : i + 1, :])
        for shift in (4, 2, 1):
            common = jnp.bitwise_xor(common, jnp.right_shift(common, shift))
        parity = jnp.bitwise_and(common, 1)
        sk[i] = (1 - 2 * parity).astype(jnp.float32).astype(jnp.bfloat16)

    pl.semaphore_wait(barrier, 8 + lax.min(zl, 1) + lax.min(chips - 1 - zl, 1))

    load_x.wait()

    z_copy = remote(own_block, own_block, z_send, z_recv, head=z_partner)
    z_copy.start()
    sent.append(z_copy)

    def line(stage, eta, phase, shift):
        first_is_y = eta == 1
        a, b = (y, x) if first_is_y else (x, y)
        zz = z if stage == 0 else 1 - z
        base = (stage * 2 + eta) * 20 + (0 if phase == 0 else 4 + 4 * shift)
        pos = a if phase == 0 else b

        def device(place):
            return head_at(z, eta, place, b, first_is_y) if phase == 0 else head_at(z, eta, a, place, first_is_y)

        def piece(place, low, count):
            if phase == 0:
                t = head_at(zz, eta, place, b, first_is_y)
            else:
                t = head_at(zz, eta, turn(a, SHIFTS[shift]), place, first_is_y)
            return xbuf.at[t, eta, pl.ds(low, count)]

        def copy(k, what, step):
            return remote(what, what, ag_send.at[base + k], ag_recv.at[base + k], head=device(turn(pos, step)))

        def send(k, what, step):
            one = copy(k, what, step)
            one.start()
            sent.append(one)

        sides = ((3, 1), (1, 3), (2, 2))

        def start():
            send(0, piece(pos, 0, HALF), 1)
            send(1, piece(pos, 0, HALF), 3)
            send(2, piece(pos, 0, HALF if phase == 0 else NEAR), 2)

        def arrive(k):
            low, goes = sides[k]
            count = NEAR if phase == 1 and k == 2 else HALF
            copy(k, piece(turn(pos, low), 0, count), goes).wait_recv()

        def relay():
            low, goes = sides[VIA]
            arrive(VIA)
            send(3, piece(turn(pos, low), NEAR, HALF - NEAR), goes)

        def finish():
            arrive(1 - VIA)
            arrive(2)
            copy(3, piece(turn(pos, 2), NEAR, HALF - NEAR), sides[VIA][1]).wait_recv()

        return start, arrive, relay, finish

    def spread(stage, fillers):
        first = [line(stage, eta, 0, 0) for eta in (0, 1)]
        second = [[line(stage, eta, 1, shift) for shift in range(4)] for eta in (0, 1)]
        for eta in (0, 1):
            first[eta][0]()
        for eta in (0, 1):
            second[eta][0][0]()
        fillers[0]()
        for k in (0, 1, 2):
            for eta in (0, 1):
                first[eta][1](k)
                second[eta][1 + k][0]()
        fillers[1]()
        for shift in range(4):
            for eta in (0, 1):
                second[eta][shift][2]()
            fillers[2 + shift]()

        def finish():
            for shift in range(4):
                for eta in (0, 1):
                    second[eta][shift][3]()

        return finish

    def project(zz, k):
        t = zz * 16 + k * RING
        part = jnp.concatenate([xbuf[t + j].reshape(BLOCK, HD) for j in range(RING)], axis=1)
        acc[...] += dot(part, wv[pl.ds(pl.multiple_of(t * HD, RING * HD), RING * HD), :])

    def idle():
        pass

    finish_own = spread(0, [idle] * 6)
    for one in load_w:
        one.wait()
    z_block = xbuf.at[z_partner]
    remote(z_block, z_block, z_send, z_recv, head=z_partner).wait_recv()
    steps = [lambda k=k: project(z, k) for k in range(RING)]
    finish_other = spread(1, [finish_own, steps[0], steps[1], steps[2], steps[3], idle])
    finish_other()
    for k in range(RING):
        project(1 - z, k)

    def normalize(raw):
        return (raw * lax.rsqrt(jnp.mean(raw * raw, axis=-1, keepdims=True) + 1e-06)).astype(jnp.bfloat16)

    factor = score_scale * score_scale / (HD * math.sqrt(QUARTER))

    def twice(normed):
        wide = normed.astype(jnp.float32)
        first = dot((wide * signed[0:1, :]).astype(jnp.bfloat16), sk[0])
        second = dot((wide * signed[1:2, :]).astype(jnp.bfloat16), sk[1])
        return factor * first * second

    kn = normalize(acc[:, HD : 2 * HD])
    kf = twice(kn)
    low_half = lax.broadcasted_iota(jnp.int32, (HALF, HD), 1) < QUARTER
    kvb[ctx, 0] = jnp.where(low_half, kf[:HALF], kf[HALF:]).astype(jnp.bfloat16)
    kvb[ctx, 1] = acc[:HALF, 2 * HD :].astype(jnp.bfloat16)
    kvb[ctx, 2] = acc[HALF:, 2 * HD :].astype(jnp.bfloat16)
    qn = normalize(acc[:, :HD])
    qd = twice(qn)
    lanes_low = lax.broadcasted_iota(jnp.int32, (BLOCK, HD), 1) < QUARTER
    qf[0] = jnp.where(lanes_low, qd, 0.0).astype(jnp.bfloat16)
    qf[1] = jnp.where(lanes_low, 0.0, qd).astype(jnp.bfloat16)

    def kv(slot, piece, sems, target):
        k = 3 * slot + piece
        return remote(kvb.at[slot, piece], kvb.at[slot, piece], sems.at[k], kv_recv.at[k], ctx=target)

    def up(slot):
        return [kv(slot, piece, kv_send, ctx + 2) for piece in range(3)]

    def over(slot):
        return [kv(slot, piece, kv_pass, other_core) for piece in range(3)]

    def values(slot):
        return kvb[slot, pl.ds(1, 2)].reshape(BLOCK, HD)

    @pl.when(zl < chips - 1)
    def _():
        for one in up(ctx):
            one.start()

    @pl.when(core == 0)
    def _():
        for one in over(ctx):
            one.start()

    scores = dot_t(qn, kn)
    causal = (
        lax.broadcasted_iota(jnp.int32, (BLOCK, BLOCK), 0)
        >= lax.broadcasted_iota(jnp.int32, (BLOCK, BLOCK), 1)
    )
    scaled = scores * (score_scale / HD)
    square = scaled * scaled
    weights = jnp.where(causal, square * square, 0.0)
    wsum[...] = weights[:, :HD] + weights[:, HD:]
    num[...] = dot(weights.astype(jnp.bfloat16), values(ctx))

    def attend(slot):
        packed = kvb[slot, 0]
        left = dot_t(qf[0], packed)
        right = dot_t(qf[1], packed)
        left = left * left
        right = right * right
        wsum[...] += left + right
        both = jnp.concatenate([left.astype(jnp.bfloat16), right.astype(jnp.bfloat16)], axis=1)
        num[...] += dot(both, values(slot))

    @pl.when(core == 1)
    def _():
        for one in over(2 * zl):
            one.wait_recv()
        attend(2 * zl)

    def earlier(s, carry):
        chip = zl - 1 - s
        slot = 2 * chip + core
        for piece in range(3):
            kv(slot, piece, kv_send, other_core).wait_recv()

            @pl.when(zl < chips - 1)
            def _():
                kv(slot, piece, kv_send, ctx + 2).start()

            kv(slot, piece, kv_pass, other_core).start()

        attend(slot)
        second = 2 * chip + 1 - core
        for one in over(second):
            one.wait_recv()
        attend(second)
        return carry

    lax.fori_loop(0, zl, earlier, 0)

    total = 1.0 + jnp.sum(wsum[...], axis=-1, keepdims=True)
    attended = (num[...] / total).astype(jnp.bfloat16)

    load_wo.wait()
    def tiles(stage, rows):
        zz = 1 - z if stage == 0 else z
        for row in rows:
            low = pl.multiple_of((zz * 16 + row * RING) * HD, RING * HD)
            product = dot(attended, wov[:, pl.ds(low, RING * HD)]).astype(jnp.bfloat16)
            for col in range(RING):
                tile = product[:, col * HD : (col + 1) * HD]
                s1[0, stage, row, col] = tile[:HALF]
                s1[1, stage, col, row] = tile[HALF:]

    tiles(0, range(RING))
    tiles(1, (0, 1))

    PAIR = RING // 2

    def ring(eta, step):
        a, b = (y, x) if eta == 0 else (x, y)
        to = turn(a, step)
        return to, head_at(z, eta, to, b, eta == 0)

    def rsa(stage, eta, side):
        k = (stage * 2 + eta) * 2 + side
        far, _ = ring(eta, 2)
        _, device = ring(eta, 1 if side == 0 else 3)
        return remote(
            s1.at[eta, stage, far, pl.ds(side * PAIR, PAIR)], ra.at[eta, stage, side],
            rsa_send.at[k], rsa_recv.at[k], head=device,
        )

    def rs1(stage, eta, side, half):
        k = ((stage * 2 + eta) * 2 + side) * 2 + half
        to, device = ring(eta, 1 if side == 0 else 3)
        return remote(
            s1.at[eta, stage, to, pl.ds(half * PAIR, PAIR)], r1.at[eta, stage, side, pl.ds(half * PAIR, PAIR)],
            rs1_send.at[k], rs1_recv.at[k], head=device,
        )

    def rs2(stage, eta, step):
        a, b = (y, x) if eta == 0 else (x, y)
        k = (stage * 2 + eta) * 3 + step - 1
        to = turn(b, step)
        return remote(
            s2.at[eta, stage, to], r2.at[eta, stage, step - 1], rs2_send.at[k], rs2_recv.at[k],
            head=head_at(z, eta, a, to, eta == 0),
        )

    def rs3(eta):
        return remote(s3.at[eta], r3.at[eta], rs3_send.at[eta], rs3_recv.at[eta], head=z_partner)

    def begin(one):
        one.start()
        sent.append(one)

    ways = [(eta, side) for eta in (0, 1) for side in (0, 1)]

    def send_first(stage):
        for eta, side in ways:
            begin(rsa(stage, eta, side))
        for eta, side in ways:
            begin(rs1(stage, eta, side, 1 - side))

    send_first(0)
    tiles(1, (2, 3))

    f32 = jnp.float32

    def relay_first(stage):
        for eta, side in ways:
            rsa(stage, eta, side).wait_recv()
            to, _ = ring(eta, 1 if side == 0 else 3)
            part = pl.ds(side * PAIR, PAIR)
            s1[eta, stage, to, part] = (
                s1[eta, stage, to, part].astype(f32) + ra[eta, stage, side].astype(f32)
            ).astype(jnp.bfloat16)
        for eta, side in ways:
            begin(rs1(stage, eta, side, side))

    def reduce_first(stage):
        for eta, side in ways:
            rs1(stage, eta, side, 1 - side).wait_recv()
        for eta, side in ways:
            rs1(stage, eta, side, side).wait_recv()
        for eta in (0, 1):
            a = y if eta == 0 else x
            for b in range(RING):
                value = s1[eta, stage, a, b].astype(f32)
                for k in range(2):
                    value = value + r1[eta, stage, k, b].astype(f32)
                s2[eta, stage, b] = value.astype(jnp.bfloat16)
        for step in (2, 1, 3):
            for eta in (0, 1):
                one = rs2(stage, eta, step)
                one.start()
                sent.append(one)

    def reduce_second(stage, eta):
        a, b = (y, x) if eta == 0 else (x, y)
        value = s1[eta, stage, a, b].astype(f32)
        for k in range(2):
            value = value + r1[eta, stage, k, b].astype(f32)
        for step in (1, 3, 2):
            rs2(stage, eta, step).wait_recv()
        for k in range(3):
            value = value + r2[eta, stage, k].astype(f32)
        return value

    relay_first(0)
    send_first(1)
    reduce_first(0)
    relay_first(1)
    for eta in (0, 1):
        s3[eta] = reduce_second(0, eta).astype(jnp.bfloat16)
    for eta in (0, 1):
        begin(rs3(eta))
    reduce_first(1)
    for eta in (0, 1):
        t1[eta] = reduce_second(1, eta)
    for eta in (0, 1):
        rs3(eta).wait_recv()
        out_ref[pl.ds(eta * HALF, HALF), :] = (t1[eta] + r3[eta].astype(f32)).astype(jnp.bfloat16)

    for one in sent:
        one.wait_send()

    @pl.when(zl < chips - 1)
    def _():
        for one in up(ctx):
            one.wait_send()

    @pl.when(core == 0)
    def _():
        for one in over(ctx):
            one.wait_send()

    def drain(s, carry):
        slot = 2 * (zl - 1 - s) + core

        @pl.when(zl < chips - 1)
        def _():
            for one in up(slot):
                one.wait_send()

        for one in over(slot):
            one.wait_send()
        return carry

    lax.fori_loop(0, zl, drain, 0)


def shards(tokens, qkv_weight, out_weight, signs, rows):
    width = qkv_weight.shape[0]
    parts = lax.axis_size("ctx")
    by_kind = qkv_weight.transpose(1, 0, 2)
    bf16, f32 = jnp.bfloat16, jnp.float32
    anywhere = pl.BlockSpec(memory_space=pl.ANY)
    vmem = pl.BlockSpec(memory_space=pltpu.VMEM)
    dma = pltpu.SemaphoreType.DMA
    return pl.pallas_call(
        kernel,
        out_shape=jax.ShapeDtypeStruct((BLOCK, HD), bf16),
        in_specs=[anywhere, anywhere, anywhere, vmem, vmem],
        out_specs=vmem,
        scratch_shapes=[
            pltpu.VMEM((width // HD, 2, HALF, HD), bf16),
            pltpu.VMEM((width, 3 * HD), bf16),
            pltpu.VMEM((HD, width), bf16),
            pltpu.VMEM((BLOCK, 3 * HD), f32),
            pltpu.VMEM((parts, 3, HALF, HD), bf16),
            pltpu.VMEM((2, HD, HD), bf16),
            pltpu.VMEM((2, BLOCK, HD), bf16),
            pltpu.VMEM((BLOCK, HD), f32),
            pltpu.VMEM((BLOCK, HD), f32),
            pltpu.VMEM((2, 2, RING, RING, HALF, HD), bf16),
            pltpu.VMEM((2, 2, 2, RING // 2, HALF, HD), bf16),
            pltpu.VMEM((2, 2, 2, RING, HALF, HD), bf16),
            pltpu.VMEM((2, 2, RING, HALF, HD), bf16),
            pltpu.VMEM((2, 2, 3, HALF, HD), bf16),
            pltpu.VMEM((2, HALF, HD), bf16),
            pltpu.VMEM((2, HALF, HD), bf16),
            pltpu.VMEM((2, HALF, HD), f32),
            dma((5,)),
            dma,
            dma,
            dma((80,)),
            dma((80,)),
            dma((3 * parts,)),
            dma((3 * parts,)),
            dma((3 * parts,)),
            dma((8,)),
            dma((8,)),
            dma((16,)),
            dma((16,)),
            dma((12,)),
            dma((12,)),
            dma((2,)),
            dma((2,)),
        ],
        compiler_params=pltpu.CompilerParams(collective_id=0, has_side_effects=True),
    )(tokens.reshape(2, HALF, HD), by_kind, out_weight, signs, rows)


def solution(mesh):
    in_specs = (
        P("ctx", "head"),
        P(None, None, "head"),
        P("head", None),
        P("head", None, None),
        P("head", None, None),
    )
    out_specs = P("ctx", "head")
    return jax.shard_map(shards, mesh=mesh, in_specs=in_specs, out_specs=out_specs, check_vma=False)
```

```python
import math

import jax
import jax.numpy as jnp
from jax import lax
from jax.experimental import pallas as pl
from jax.experimental.pallas import tpu as pltpu
from jax.sharding import PartitionSpec as P

MESH = pl.DeviceIdType.MESH
BLOCK = 256
HALF = 128
QUARTER = 64
HD = 128
NEAR = 64
VIA = 1
RING = 4
SHIFTS = (0, 3, 1, 2)

score_scale = 2.0


def dot(left, right):
    return jnp.dot(left, right, preferred_element_type=jnp.float32)


def dot_t(left, right):
    return lax.dot_general(left, right, (((1,), (1,)), ((), ())), preferred_element_type=jnp.float32)


def turn(place, step):
    return lax.rem(place + step, RING)


def kernel(
    x_ref, w_ref, wo_ref, signs_ref, rows_ref, out_ref,
    xbuf, wv, wov, acc, kvb, sk, qf, num, wsum,
    s1, ra, r1, s2, r2, s3, r3, t1,
    load_sem, z_send, z_recv, ag_send, ag_recv,
    kv_send, kv_pass, kv_recv, rsa_send, rsa_recv, rs1_send, rs1_recv, rs2_send, rs2_recv, rs3_send, rs3_recv,
):
    head = lax.axis_index("head")
    ctx = lax.axis_index("ctx")
    chips = lax.axis_size("ctx") // 2
    z = lax.div(head, RING * RING)
    y = lax.rem(lax.div(head, RING), RING)
    x = lax.rem(head, RING)
    zl = lax.div(ctx, 2)
    core = lax.rem(ctx, 2)
    other_core = ctx + 1 - 2 * core
    z_partner = (1 - z) * RING * RING + y * RING + x
    sent = []

    def remote(src, dst, send_sem, recv_sem, **device):
        return pltpu.make_async_remote_copy(
            src_ref=src, dst_ref=dst, send_sem=send_sem, recv_sem=recv_sem,
            device_id=device, device_id_type=MESH,
        )

    def head_at(zz, eta, a, b, first_is_y):
        if first_is_y:
            return zz * RING * RING + a * RING + b
        return zz * RING * RING + b * RING + a

    own_block = xbuf.at[head]
    load_x = pltpu.make_async_copy(x_ref, own_block, load_sem.at[0])
    load_w = [
        pltpu.make_async_copy(w_ref.at[j], wv.at[:, pl.ds(j * HD, HD)], load_sem.at[2 + j])
        for j in range(3)
    ]
    load_wo = pltpu.make_async_copy(wo_ref, wov, load_sem.at[1])
    load_x.start()
    for one in load_w:
        one.start()
    load_wo.start()
    barrier = pltpu.get_barrier_semaphore()
    for step in (1, 2, 3):
        for place in (z * 16 + y * RING + turn(x, step), z * 16 + turn(y, step) * RING + x):
            pl.semaphore_signal(barrier, inc=1, device_id={"head": place}, device_id_type=MESH)
    pl.semaphore_signal(barrier, inc=1, device_id={"head": z_partner}, device_id_type=MESH)
    pl.semaphore_signal(barrier, inc=1, device_id={"ctx": other_core}, device_id_type=MESH)

    @pl.when(zl > 0)
    def _():
        pl.semaphore_signal(barrier, inc=1, device_id={"ctx": ctx - 2}, device_id_type=MESH)

    @pl.when(zl < chips - 1)
    def _():
        pl.semaphore_signal(barrier, inc=1, device_id={"ctx": ctx + 2}, device_id_type=MESH)

    acc[...] = jnp.zeros_like(acc)

    signed = (2 * signs_ref[0] - 1).astype(jnp.float32)
    sampled = jnp.concatenate([rows_ref[0], rows_ref[0]], axis=1)
    entry = lax.broadcasted_iota(jnp.int32, (HD, HD), 0)
    for i in (0, 1):
        common = jnp.bitwise_and(entry, sampled[i : i + 1, :])
        for shift in (4, 2, 1):
            common = jnp.bitwise_xor(common, jnp.right_shift(common, shift))
        parity = jnp.bitwise_and(common, 1)
        sk[i] = (1 - 2 * parity).astype(jnp.float32).astype(jnp.bfloat16)

    pl.semaphore_wait(barrier, 8 + lax.min(zl, 1) + lax.min(chips - 1 - zl, 1))

    load_x.wait()

    z_copy = remote(own_block, own_block, z_send, z_recv, head=z_partner)
    z_copy.start()
    sent.append(z_copy)

    def line(stage, eta, phase, shift):
        first_is_y = eta == 1
        a, b = (y, x) if first_is_y else (x, y)
        zz = z if stage == 0 else 1 - z
        base = (stage * 2 + eta) * 20 + (0 if phase == 0 else 4 + 4 * shift)
        pos = a if phase == 0 else b

        def device(place):
            return head_at(z, eta, place, b, first_is_y) if phase == 0 else head_at(z, eta, a, place, first_is_y)

        def piece(place, low, count):
            if phase == 0:
                t = head_at(zz, eta, place, b, first_is_y)
            else:
                t = head_at(zz, eta, turn(a, SHIFTS[shift]), place, first_is_y)
            return xbuf.at[t, eta, pl.ds(low, count)]

        def copy(k, what, step):
            return remote(what, what, ag_send.at[base + k], ag_recv.at[base + k], head=device(turn(pos, step)))

        def send(k, what, step):
            one = copy(k, what, step)
            one.start()
            sent.append(one)

        sides = ((3, 1), (1, 3), (2, 2))

        def start():
            send(0, piece(pos, 0, HALF), 1)
            send(1, piece(pos, 0, HALF), 3)
            send(2, piece(pos, 0, HALF if phase == 0 else NEAR), 2)

        def arrive(k):
            low, goes = sides[k]
            count = NEAR if phase == 1 and k == 2 else HALF
            copy(k, piece(turn(pos, low), 0, count), goes).wait_recv()

        def relay():
            low, goes = sides[VIA]
            arrive(VIA)
            send(3, piece(turn(pos, low), NEAR, HALF - NEAR), goes)

        def finish():
            arrive(1 - VIA)
            arrive(2)
            copy(3, piece(turn(pos, 2), NEAR, HALF - NEAR), sides[VIA][1]).wait_recv()

        return start, arrive, relay, finish

    def spread(stage, fillers):
        first = [line(stage, eta, 0, 0) for eta in (0, 1)]
        second = [[line(stage, eta, 1, shift) for shift in range(4)] for eta in (0, 1)]
        for eta in (0, 1):
            first[eta][0]()
        for eta in (0, 1):
            second[eta][0][0]()
        fillers[0]()
        for k in (0, 1, 2):
            for eta in (0, 1):
                first[eta][1](k)
                second[eta][1 + k][0]()
        fillers[1]()
        for shift in range(4):
            for eta in (0, 1):
                second[eta][shift][2]()
            fillers[2 + shift]()

        def finish():
            for shift in range(4):
                for eta in (0, 1):
                    second[eta][shift][3]()

        return finish

    def project(zz, k, low=0, high=3 * HD):
        t = zz * 16 + k * RING
        part = jnp.concatenate([xbuf[t + j].reshape(BLOCK, HD) for j in range(RING)], axis=1)
        deep = pl.ds(pl.multiple_of(t * HD, RING * HD), RING * HD)
        acc[:, low:high] += dot(part, wv[deep, low:high])

    def idle():
        pass

    finish_own = spread(0, [idle] * 6)
    for one in load_w:
        one.wait()
    z_block = xbuf.at[z_partner]
    remote(z_block, z_block, z_send, z_recv, head=z_partner).wait_recv()
    steps = [lambda k=k: project(z, k) for k in range(RING)]
    finish_other = spread(1, [finish_own, steps[0], steps[1], steps[2], steps[3], idle])
    finish_other()
    for k in range(RING):
        project(1 - z, k, HD)

    def normalize(raw):
        return (raw * lax.rsqrt(jnp.mean(raw * raw, axis=-1, keepdims=True) + 1e-06)).astype(jnp.bfloat16)

    factor = score_scale * score_scale / (HD * math.sqrt(QUARTER))

    def twice(normed):
        wide = normed.astype(jnp.float32)
        first = dot((wide * signed[0:1, :]).astype(jnp.bfloat16), sk[0])
        second = dot((wide * signed[1:2, :]).astype(jnp.bfloat16), sk[1])
        return factor * first * second

    kn = normalize(acc[:, HD : 2 * HD])
    kf = twice(kn)
    low_half = lax.broadcasted_iota(jnp.int32, (HALF, HD), 1) < QUARTER
    kvb[ctx, 0] = jnp.where(low_half, kf[:HALF], kf[HALF:]).astype(jnp.bfloat16)
    kvb[ctx, 1] = acc[:HALF, 2 * HD :].astype(jnp.bfloat16)
    kvb[ctx, 2] = acc[HALF:, 2 * HD :].astype(jnp.bfloat16)
    for k in range(RING):
        project(1 - z, k, 0, HD)

    def kv(slot, piece, sems, target):
        k = 3 * slot + piece
        return remote(kvb.at[slot, piece], kvb.at[slot, piece], sems.at[k], kv_recv.at[k], ctx=target)

    def up(slot):
        return [kv(slot, piece, kv_send, ctx + 2) for piece in range(3)]

    def over(slot):
        return [kv(slot, piece, kv_pass, other_core) for piece in range(3)]

    def values(slot):
        return kvb[slot, pl.ds(1, 2)].reshape(BLOCK, HD)

    @pl.when(zl < chips - 1)
    def _():
        for one in up(ctx):
            one.start()

    @pl.when(core == 0)
    def _():
        for one in over(ctx):
            one.start()

    qn = normalize(acc[:, :HD])
    qd = twice(qn)
    lanes_low = lax.broadcasted_iota(jnp.int32, (BLOCK, HD), 1) < QUARTER
    qf[0] = jnp.where(lanes_low, qd, 0.0).astype(jnp.bfloat16)
    qf[1] = jnp.where(lanes_low, 0.0, qd).astype(jnp.bfloat16)

    scores = dot_t(qn, kn)
    causal = (
        lax.broadcasted_iota(jnp.int32, (BLOCK, BLOCK), 0)
        >= lax.broadcasted_iota(jnp.int32, (BLOCK, BLOCK), 1)
    )
    scaled = scores * (score_scale / HD)
    square = scaled * scaled
    weights = jnp.where(causal, square * square, 0.0)
    wsum[...] = weights[:, :HD] + weights[:, HD:]
    num[...] = dot(weights.astype(jnp.bfloat16), values(ctx))

    def attend(slot):
        packed = kvb[slot, 0]
        left = dot_t(qf[0], packed)
        right = dot_t(qf[1], packed)
        left = left * left
        right = right * right
        wsum[...] += left + right
        both = jnp.concatenate([left.astype(jnp.bfloat16), right.astype(jnp.bfloat16)], axis=1)
        num[...] += dot(both, values(slot))

    @pl.when(core == 1)
    def _():
        for one in over(2 * zl):
            one.wait_recv()
        attend(2 * zl)

    def earlier(s, carry):
        chip = zl - 1 - s
        slot = 2 * chip + core
        for piece in range(3):
            kv(slot, piece, kv_send, other_core).wait_recv()

            @pl.when(zl < chips - 1)
            def _():
                kv(slot, piece, kv_send, ctx + 2).start()

            kv(slot, piece, kv_pass, other_core).start()

        attend(slot)
        second = 2 * chip + 1 - core
        for one in over(second):
            one.wait_recv()
        attend(second)
        return carry

    lax.fori_loop(0, zl, earlier, 0)

    total = 1.0 + jnp.sum(wsum[...], axis=-1, keepdims=True)
    attended = (num[...] / total).astype(jnp.bfloat16)

    load_wo.wait()
    def tiles(stage, rows):
        zz = 1 - z if stage == 0 else z
        for row in rows:
            low = pl.multiple_of((zz * 16 + row * RING) * HD, RING * HD)
            product = dot(attended, wov[:, pl.ds(low, RING * HD)]).astype(jnp.bfloat16)
            for col in range(RING):
                tile = product[:, col * HD : (col + 1) * HD]
                s1[0, stage, row, col] = tile[:HALF]
                s1[1, stage, col, row] = tile[HALF:]

    tiles(0, range(RING))
    tiles(1, (0, 1))

    PAIR = RING // 2

    def ring(eta, step):
        a, b = (y, x) if eta == 0 else (x, y)
        to = turn(a, step)
        return to, head_at(z, eta, to, b, eta == 0)

    def rsa(stage, eta, side):
        k = (stage * 2 + eta) * 2 + side
        far, _ = ring(eta, 2)
        _, device = ring(eta, 1 if side == 0 else 3)
        return remote(
            s1.at[eta, stage, far, pl.ds(side * PAIR, PAIR)], ra.at[eta, stage, side],
            rsa_send.at[k], rsa_recv.at[k], head=device,
        )

    def rs1(stage, eta, side, half):
        k = ((stage * 2 + eta) * 2 + side) * 2 + half
        to, device = ring(eta, 1 if side == 0 else 3)
        return remote(
            s1.at[eta, stage, to, pl.ds(half * PAIR, PAIR)], r1.at[eta, stage, side, pl.ds(half * PAIR, PAIR)],
            rs1_send.at[k], rs1_recv.at[k], head=device,
        )

    def rs2(stage, eta, step):
        a, b = (y, x) if eta == 0 else (x, y)
        k = (stage * 2 + eta) * 3 + step - 1
        to = turn(b, step)
        return remote(
            s2.at[eta, stage, to], r2.at[eta, stage, step - 1], rs2_send.at[k], rs2_recv.at[k],
            head=head_at(z, eta, a, to, eta == 0),
        )

    def rs3(eta):
        return remote(s3.at[eta], r3.at[eta], rs3_send.at[eta], rs3_recv.at[eta], head=z_partner)

    def begin(one):
        one.start()
        sent.append(one)

    ways = [(eta, side) for eta in (0, 1) for side in (0, 1)]

    def send_first(stage):
        for eta, side in ways:
            begin(rsa(stage, eta, side))
        for eta, side in ways:
            begin(rs1(stage, eta, side, 1 - side))

    send_first(0)
    tiles(1, (2, 3))

    f32 = jnp.float32

    def relay_first(stage):
        for eta, side in ways:
            rsa(stage, eta, side).wait_recv()
            to, _ = ring(eta, 1 if side == 0 else 3)
            part = pl.ds(side * PAIR, PAIR)
            s1[eta, stage, to, part] = (
                s1[eta, stage, to, part].astype(f32) + ra[eta, stage, side].astype(f32)
            ).astype(jnp.bfloat16)
        for eta, side in ways:
            begin(rs1(stage, eta, side, side))

    def reduce_first(stage):
        for eta, side in ways:
            rs1(stage, eta, side, 1 - side).wait_recv()
        for eta, side in ways:
            rs1(stage, eta, side, side).wait_recv()
        for eta in (0, 1):
            a = y if eta == 0 else x
            for b in range(RING):
                value = s1[eta, stage, a, b].astype(f32)
                for k in range(2):
                    value = value + r1[eta, stage, k, b].astype(f32)
                s2[eta, stage, b] = value.astype(jnp.bfloat16)
        for step in (2, 1, 3):
            for eta in (0, 1):
                one = rs2(stage, eta, step)
                one.start()
                sent.append(one)

    def reduce_second(stage, eta):
        a, b = (y, x) if eta == 0 else (x, y)
        value = s1[eta, stage, a, b].astype(f32)
        for k in range(2):
            value = value + r1[eta, stage, k, b].astype(f32)
        for step in (1, 3, 2):
            rs2(stage, eta, step).wait_recv()
        for k in range(3):
            value = value + r2[eta, stage, k].astype(f32)
        return value

    relay_first(0)
    send_first(1)
    reduce_first(0)
    relay_first(1)
    for eta in (0, 1):
        s3[eta] = reduce_second(0, eta).astype(jnp.bfloat16)
    for eta in (0, 1):
        begin(rs3(eta))
    reduce_first(1)
    for eta in (0, 1):
        t1[eta] = reduce_second(1, eta)
    for eta in (0, 1):
        rs3(eta).wait_recv()
        out_ref[pl.ds(eta * HALF, HALF), :] = (t1[eta] + r3[eta].astype(f32)).astype(jnp.bfloat16)

    for one in sent:
        one.wait_send()

    @pl.when(zl < chips - 1)
    def _():
        for one in up(ctx):
            one.wait_send()

    @pl.when(core == 0)
    def _():
        for one in over(ctx):
            one.wait_send()

    def drain(s, carry):
        slot = 2 * (zl - 1 - s) + core

        @pl.when(zl < chips - 1)
        def _():
            for one in up(slot):
                one.wait_send()

        for one in over(slot):
            one.wait_send()
        return carry

    lax.fori_loop(0, zl, drain, 0)


def shards(tokens, qkv_weight, out_weight, signs, rows):
    width = qkv_weight.shape[0]
    parts = lax.axis_size("ctx")
    by_kind = qkv_weight.transpose(1, 0, 2)
    bf16, f32 = jnp.bfloat16, jnp.float32
    anywhere = pl.BlockSpec(memory_space=pl.ANY)
    vmem = pl.BlockSpec(memory_space=pltpu.VMEM)
    dma = pltpu.SemaphoreType.DMA
    return pl.pallas_call(
        kernel,
        out_shape=jax.ShapeDtypeStruct((BLOCK, HD), bf16),
        in_specs=[anywhere, anywhere, anywhere, vmem, vmem],
        out_specs=vmem,
        scratch_shapes=[
            pltpu.VMEM((width // HD, 2, HALF, HD), bf16),
            pltpu.VMEM((width, 3 * HD), bf16),
            pltpu.VMEM((HD, width), bf16),
            pltpu.VMEM((BLOCK, 3 * HD), f32),
            pltpu.VMEM((parts, 3, HALF, HD), bf16),
            pltpu.VMEM((2, HD, HD), bf16),
            pltpu.VMEM((2, BLOCK, HD), bf16),
            pltpu.VMEM((BLOCK, HD), f32),
            pltpu.VMEM((BLOCK, HD), f32),
            pltpu.VMEM((2, 2, RING, RING, HALF, HD), bf16),
            pltpu.VMEM((2, 2, 2, RING // 2, HALF, HD), bf16),
            pltpu.VMEM((2, 2, 2, RING, HALF, HD), bf16),
            pltpu.VMEM((2, 2, RING, HALF, HD), bf16),
            pltpu.VMEM((2, 2, 3, HALF, HD), bf16),
            pltpu.VMEM((2, HALF, HD), bf16),
            pltpu.VMEM((2, HALF, HD), bf16),
            pltpu.VMEM((2, HALF, HD), f32),
            dma((5,)),
            dma,
            dma,
            dma((80,)),
            dma((80,)),
            dma((3 * parts,)),
            dma((3 * parts,)),
            dma((3 * parts,)),
            dma((8,)),
            dma((8,)),
            dma((16,)),
            dma((16,)),
            dma((12,)),
            dma((12,)),
            dma((2,)),
            dma((2,)),
        ],
        compiler_params=pltpu.CompilerParams(collective_id=0, has_side_effects=True),
    )(tokens.reshape(2, HALF, HD), by_kind, out_weight, signs, rows)


def solution(mesh):
    in_specs = (
        P("ctx", "head"),
        P(None, None, "head"),
        P("head", None),
        P("head", None, None),
        P("head", None, None),
    )
    out_specs = P("ctx", "head")
    return jax.shard_map(shards, mesh=mesh, in_specs=in_specs, out_specs=out_specs, check_vma=False)
```

```python
import math

import jax
import jax.numpy as jnp
from jax import lax
from jax.experimental import pallas as pl
from jax.experimental.pallas import tpu as pltpu
from jax.sharding import PartitionSpec as P

MESH = pl.DeviceIdType.MESH
BLOCK = 256
HALF = 128
QUARTER = 64
HD = 128
NEAR = 64
VIA = 1
RING = 4
SHIFTS = (0, 3, 1, 2)

score_scale = 2.0


def dot(left, right):
    return jnp.dot(left, right, preferred_element_type=jnp.float32)


def dot_t(left, right):
    return lax.dot_general(left, right, (((1,), (1,)), ((), ())), preferred_element_type=jnp.float32)


def turn(place, step):
    return lax.rem(place + step, RING)


def kernel(
    x_ref, w_ref, wo_ref, signs_ref, rows_ref, out_ref,
    xbuf, wv, wov, acc, kvb, sk, qf, num, wsum,
    s1, ra, r1, s2, r2, s3, r3, t1,
    load_sem, z_send, z_recv, ag_send, ag_recv,
    kv_send, kv_pass, kv_recv, rsa_send, rsa_recv, rs1_send, rs1_recv, rs2_send, rs2_recv, rs3_send, rs3_recv,
):
    head = lax.axis_index("head")
    ctx = lax.axis_index("ctx")
    chips = lax.axis_size("ctx") // 2
    z = lax.div(head, RING * RING)
    y = lax.rem(lax.div(head, RING), RING)
    x = lax.rem(head, RING)
    zl = lax.div(ctx, 2)
    core = lax.rem(ctx, 2)
    other_core = ctx + 1 - 2 * core
    z_partner = (1 - z) * RING * RING + y * RING + x
    sent = []

    def remote(src, dst, send_sem, recv_sem, **device):
        return pltpu.make_async_remote_copy(
            src_ref=src, dst_ref=dst, send_sem=send_sem, recv_sem=recv_sem,
            device_id=device, device_id_type=MESH,
        )

    def head_at(zz, eta, a, b, first_is_y):
        if first_is_y:
            return zz * RING * RING + a * RING + b
        return zz * RING * RING + b * RING + a

    own_block = xbuf.at[head]
    load_x = pltpu.make_async_copy(x_ref, own_block, load_sem.at[0])
    load_w = [
        pltpu.make_async_copy(w_ref.at[j], wv.at[:, pl.ds(j * HD, HD)], load_sem.at[2 + j])
        for j in range(3)
    ]
    load_wo = pltpu.make_async_copy(wo_ref, wov, load_sem.at[1])
    load_x.start()
    for one in load_w:
        one.start()
    load_wo.start()
    barrier = pltpu.get_barrier_semaphore()
    for step in (1, 2, 3):
        for place in (z * 16 + y * RING + turn(x, step), z * 16 + turn(y, step) * RING + x):
            pl.semaphore_signal(barrier, inc=1, device_id={"head": place}, device_id_type=MESH)
    pl.semaphore_signal(barrier, inc=1, device_id={"head": z_partner}, device_id_type=MESH)
    pl.semaphore_signal(barrier, inc=1, device_id={"ctx": other_core}, device_id_type=MESH)

    @pl.when(zl > 0)
    def _():
        pl.semaphore_signal(barrier, inc=1, device_id={"ctx": ctx - 2}, device_id_type=MESH)

    @pl.when(zl < chips - 1)
    def _():
        pl.semaphore_signal(barrier, inc=1, device_id={"ctx": ctx + 2}, device_id_type=MESH)

    acc[...] = jnp.zeros_like(acc)

    signed = (2 * signs_ref[0] - 1).astype(jnp.float32)
    sampled = jnp.concatenate([rows_ref[0], rows_ref[0]], axis=1)
    entry = lax.broadcasted_iota(jnp.int32, (HD, HD), 0)
    for i in (0, 1):
        common = jnp.bitwise_and(entry, sampled[i : i + 1, :])
        for shift in (4, 2, 1):
            common = jnp.bitwise_xor(common, jnp.right_shift(common, shift))
        parity = jnp.bitwise_and(common, 1)
        sk[i] = (1 - 2 * parity).astype(jnp.float32).astype(jnp.bfloat16)

    pl.semaphore_wait(barrier, 8 + lax.min(zl, 1) + lax.min(chips - 1 - zl, 1))

    load_x.wait()

    z_copy = remote(own_block, own_block, z_send, z_recv, head=z_partner)
    z_copy.start()
    sent.append(z_copy)

    def line(stage, eta, phase, shift):
        first_is_y = eta == 1
        a, b = (y, x) if first_is_y else (x, y)
        zz = z if stage == 0 else 1 - z
        base = (stage * 2 + eta) * 20 + (0 if phase == 0 else 4 + 4 * shift)
        pos = a if phase == 0 else b

        def device(place):
            return head_at(z, eta, place, b, first_is_y) if phase == 0 else head_at(z, eta, a, place, first_is_y)

        def piece(place, low, count):
            if phase == 0:
                t = head_at(zz, eta, place, b, first_is_y)
            else:
                t = head_at(zz, eta, turn(a, SHIFTS[shift]), place, first_is_y)
            return xbuf.at[t, eta, pl.ds(low, count)]

        def copy(k, what, step):
            return remote(what, what, ag_send.at[base + k], ag_recv.at[base + k], head=device(turn(pos, step)))

        def send(k, what, step):
            one = copy(k, what, step)
            one.start()
            sent.append(one)

        sides = ((3, 1), (1, 3), (2, 2))

        def start():
            send(0, piece(pos, 0, HALF), 1)
            send(1, piece(pos, 0, HALF), 3)
            send(2, piece(pos, 0, HALF if phase == 0 else NEAR), 2)

        def arrive(k):
            low, goes = sides[k]
            count = NEAR if phase == 1 and k == 2 else HALF
            copy(k, piece(turn(pos, low), 0, count), goes).wait_recv()

        def relay():
            low, goes = sides[VIA]
            arrive(VIA)
            send(3, piece(turn(pos, low), NEAR, HALF - NEAR), goes)

        def finish():
            arrive(1 - VIA)
            arrive(2)
            copy(3, piece(turn(pos, 2), NEAR, HALF - NEAR), sides[VIA][1]).wait_recv()

        return start, arrive, relay, finish

    def spread(stage, fillers):
        first = [line(stage, eta, 0, 0) for eta in (0, 1)]
        second = [[line(stage, eta, 1, shift) for shift in range(4)] for eta in (0, 1)]
        for eta in (0, 1):
            first[eta][0]()
        for eta in (0, 1):
            second[eta][0][0]()
        fillers[0]()
        for k in (0, 1, 2):
            for eta in (0, 1):
                first[eta][1](k)
                second[eta][1 + k][0]()
        fillers[1]()
        for shift in range(4):
            for eta in (0, 1):
                second[eta][shift][2]()
            fillers[2 + shift]()

        def finish():
            for shift in range(4):
                for eta in (0, 1):
                    second[eta][shift][3]()

        return finish

    def project(zz, k, low=0, high=3 * HD):
        t = zz * 16 + k * RING
        part = jnp.concatenate([xbuf[t + j].reshape(BLOCK, HD) for j in range(RING)], axis=1)
        deep = pl.ds(pl.multiple_of(t * HD, RING * HD), RING * HD)
        acc[:, low:high] += dot(part, wv[deep, low:high])

    def idle():
        pass

    finish_own = spread(0, [idle] * 6)
    for one in load_w:
        one.wait()
    z_block = xbuf.at[z_partner]
    remote(z_block, z_block, z_send, z_recv, head=z_partner).wait_recv()
    steps = [lambda k=k: project(z, k) for k in range(RING)]
    finish_other = spread(1, [finish_own, steps[0], steps[1], steps[2], steps[3], idle])
    finish_other()
    for k in range(RING):
        project(1 - z, k, HD)

    def normalize(raw):
        return (raw * lax.rsqrt(jnp.mean(raw * raw, axis=-1, keepdims=True) + 1e-06)).astype(jnp.bfloat16)

    factor = score_scale * score_scale / (HD * math.sqrt(QUARTER))

    def twice(normed):
        wide = normed.astype(jnp.float32)
        first = dot((wide * signed[0:1, :]).astype(jnp.bfloat16), sk[0])
        second = dot((wide * signed[1:2, :]).astype(jnp.bfloat16), sk[1])
        return factor * first * second

    kn = normalize(acc[:, HD : 2 * HD])
    kf = twice(kn)
    low_half = lax.broadcasted_iota(jnp.int32, (HALF, HD), 1) < QUARTER
    kvb[ctx, 0] = jnp.where(low_half, kf[:HALF], kf[HALF:]).astype(jnp.bfloat16)
    kvb[ctx, 1] = acc[:HALF, 2 * HD :].astype(jnp.bfloat16)
    kvb[ctx, 2] = acc[HALF:, 2 * HD :].astype(jnp.bfloat16)
    for k in range(RING):
        project(1 - z, k, 0, HD)

    def kv(slot, piece, sems, target):
        k = 3 * slot + piece
        return remote(kvb.at[slot, piece], kvb.at[slot, piece], sems.at[k], kv_recv.at[k], ctx=target)

    def up(slot):
        return [kv(slot, piece, kv_send, ctx + 2) for piece in range(3)]

    def over(slot):
        return [kv(slot, piece, kv_pass, other_core) for piece in range(3)]

    def values(slot):
        return kvb[slot, pl.ds(1, 2)].reshape(BLOCK, HD)

    @pl.when(zl < chips - 1)
    def _():
        for one in up(ctx):
            one.start()

    @pl.when(core == 0)
    def _():
        for one in over(ctx):
            one.start()

    qn = normalize(acc[:, :HD])
    qd = twice(qn)
    lanes_low = lax.broadcasted_iota(jnp.int32, (BLOCK, HD), 1) < QUARTER
    qf[0] = jnp.where(lanes_low, qd, 0.0).astype(jnp.bfloat16)
    qf[1] = jnp.where(lanes_low, 0.0, qd).astype(jnp.bfloat16)

    scores = dot_t(qn, kn)
    causal = (
        lax.broadcasted_iota(jnp.int32, (BLOCK, BLOCK), 0)
        >= lax.broadcasted_iota(jnp.int32, (BLOCK, BLOCK), 1)
    )
    scaled = scores * (score_scale / HD)
    square = scaled * scaled
    weights = jnp.where(causal, square * square, 0.0)
    wsum[...] = weights[:, :HD] + weights[:, HD:]
    num[...] = dot(weights.astype(jnp.bfloat16), values(ctx))

    def attend(slot):
        packed = kvb[slot, 0]
        left = dot_t(qf[0], packed)
        right = dot_t(qf[1], packed)
        left = left * left
        right = right * right
        wsum[...] += left + right
        both = jnp.concatenate([left.astype(jnp.bfloat16), right.astype(jnp.bfloat16)], axis=1)
        num[...] += dot(both, values(slot))

    def attend_pair(chip):
        for one in over(2 * chip + 1 - core):
            one.wait_recv()
        packed = jnp.concatenate([kvb[2 * chip, 0], kvb[2 * chip + 1, 0]], axis=0)
        left = dot_t(qf[0], packed)
        right = dot_t(qf[1], packed)
        left = left * left
        right = right * right
        wsum[...] += (left[:, :HD] + right[:, :HD]) + (left[:, HD:] + right[:, HD:])
        left = left.astype(jnp.bfloat16)
        right = right.astype(jnp.bfloat16)
        both = jnp.concatenate([left[:, :HD], right[:, :HD], left[:, HD:], right[:, HD:]], axis=1)
        pair = jnp.concatenate([values(2 * chip), values(2 * chip + 1)], axis=0)
        num[...] += dot(both, pair)

    @pl.when(core == 1)
    def _():
        for one in over(2 * zl):
            one.wait_recv()
        attend(2 * zl)

    def earlier(s, carry):
        chip = zl - 1 - s
        slot = 2 * chip + core
        for piece in range(3):
            kv(slot, piece, kv_send, other_core).wait_recv()

            @pl.when(zl < chips - 1)
            def _():
                kv(slot, piece, kv_send, ctx + 2).start()

            kv(slot, piece, kv_pass, other_core).start()

        @pl.when(s > 0)
        def _():
            attend_pair(chip + 1)

        return carry

    lax.fori_loop(0, zl, earlier, 0)

    @pl.when(zl > 0)
    def _():
        attend_pair(0)

    total = 1.0 + jnp.sum(wsum[...], axis=-1, keepdims=True)
    attended = (num[...] / total).astype(jnp.bfloat16)

    load_wo.wait()
    def tiles(stage, rows):
        zz = 1 - z if stage == 0 else z
        for row in rows:
            low = pl.multiple_of((zz * 16 + row * RING) * HD, RING * HD)
            product = dot(attended, wov[:, pl.ds(low, RING * HD)]).astype(jnp.bfloat16)
            for col in range(RING):
                tile = product[:, col * HD : (col + 1) * HD]
                s1[0, stage, row, col] = tile[:HALF]
                s1[1, stage, col, row] = tile[HALF:]

    tiles(0, range(RING))
    tiles(1, (0, 1))

    PAIR = RING // 2

    def ring(eta, step):
        a, b = (y, x) if eta == 0 else (x, y)
        to = turn(a, step)
        return to, head_at(z, eta, to, b, eta == 0)

    def rsa(stage, eta, side):
        k = (stage * 2 + eta) * 2 + side
        far, _ = ring(eta, 2)
        _, device = ring(eta, 1 if side == 0 else 3)
        return remote(
            s1.at[eta, stage, far, pl.ds(side * PAIR, PAIR)], ra.at[eta, stage, side],
            rsa_send.at[k], rsa_recv.at[k], head=device,
        )

    def rs1(stage, eta, side, half):
        k = ((stage * 2 + eta) * 2 + side) * 2 + half
        to, device = ring(eta, 1 if side == 0 else 3)
        return remote(
            s1.at[eta, stage, to, pl.ds(half * PAIR, PAIR)], r1.at[eta, stage, side, pl.ds(half * PAIR, PAIR)],
            rs1_send.at[k], rs1_recv.at[k], head=device,
        )

    def rs2(stage, eta, step):
        a, b = (y, x) if eta == 0 else (x, y)
        k = (stage * 2 + eta) * 3 + step - 1
        to = turn(b, step)
        return remote(
            s2.at[eta, stage, to], r2.at[eta, stage, step - 1], rs2_send.at[k], rs2_recv.at[k],
            head=head_at(z, eta, a, to, eta == 0),
        )

    def rs3(eta):
        return remote(s3.at[eta], r3.at[eta], rs3_send.at[eta], rs3_recv.at[eta], head=z_partner)

    def begin(one):
        one.start()
        sent.append(one)

    ways = [(eta, side) for eta in (0, 1) for side in (0, 1)]

    def send_first(stage):
        for eta, side in ways:
            begin(rsa(stage, eta, side))
        for eta, side in ways:
            begin(rs1(stage, eta, side, 1 - side))

    send_first(0)
    tiles(1, (2, 3))

    f32 = jnp.float32

    def relay_first(stage):
        for eta, side in ways:
            rsa(stage, eta, side).wait_recv()
            to, _ = ring(eta, 1 if side == 0 else 3)
            part = pl.ds(side * PAIR, PAIR)
            s1[eta, stage, to, part] = (
                s1[eta, stage, to, part].astype(f32) + ra[eta, stage, side].astype(f32)
            ).astype(jnp.bfloat16)
        for eta, side in ways:
            begin(rs1(stage, eta, side, side))

    def reduce_first(stage):
        for eta, side in ways:
            rs1(stage, eta, side, 1 - side).wait_recv()
        for eta, side in ways:
            rs1(stage, eta, side, side).wait_recv()
        for eta in (0, 1):
            a = y if eta == 0 else x
            for b in range(RING):
                value = s1[eta, stage, a, b].astype(f32)
                for k in range(2):
                    value = value + r1[eta, stage, k, b].astype(f32)
                s2[eta, stage, b] = value.astype(jnp.bfloat16)
        for step in (2, 1, 3):
            for eta in (0, 1):
                one = rs2(stage, eta, step)
                one.start()
                sent.append(one)

    def reduce_second(stage, eta):
        a, b = (y, x) if eta == 0 else (x, y)
        value = s1[eta, stage, a, b].astype(f32)
        for k in range(2):
            value = value + r1[eta, stage, k, b].astype(f32)
        for step in (1, 3, 2):
            rs2(stage, eta, step).wait_recv()
        for k in range(3):
            value = value + r2[eta, stage, k].astype(f32)
        return value

    relay_first(0)
    send_first(1)
    reduce_first(0)
    relay_first(1)
    for eta in (0, 1):
        s3[eta] = reduce_second(0, eta).astype(jnp.bfloat16)
    for eta in (0, 1):
        begin(rs3(eta))
    reduce_first(1)
    for eta in (0, 1):
        t1[eta] = reduce_second(1, eta)
    for eta in (0, 1):
        rs3(eta).wait_recv()
        out_ref[pl.ds(eta * HALF, HALF), :] = (t1[eta] + r3[eta].astype(f32)).astype(jnp.bfloat16)

    for one in sent:
        one.wait_send()

    @pl.when(zl < chips - 1)
    def _():
        for one in up(ctx):
            one.wait_send()

    @pl.when(core == 0)
    def _():
        for one in over(ctx):
            one.wait_send()

    def drain(s, carry):
        slot = 2 * (zl - 1 - s) + core

        @pl.when(zl < chips - 1)
        def _():
            for one in up(slot):
                one.wait_send()

        for one in over(slot):
            one.wait_send()
        return carry

    lax.fori_loop(0, zl, drain, 0)


def shards(tokens, qkv_weight, out_weight, signs, rows):
    width = qkv_weight.shape[0]
    parts = lax.axis_size("ctx")
    by_kind = qkv_weight.transpose(1, 0, 2)
    bf16, f32 = jnp.bfloat16, jnp.float32
    anywhere = pl.BlockSpec(memory_space=pl.ANY)
    vmem = pl.BlockSpec(memory_space=pltpu.VMEM)
    dma = pltpu.SemaphoreType.DMA
    return pl.pallas_call(
        kernel,
        out_shape=jax.ShapeDtypeStruct((BLOCK, HD), bf16),
        in_specs=[anywhere, anywhere, anywhere, vmem, vmem],
        out_specs=vmem,
        scratch_shapes=[
            pltpu.VMEM((width // HD, 2, HALF, HD), bf16),
            pltpu.VMEM((width, 3 * HD), bf16),
            pltpu.VMEM((HD, width), bf16),
            pltpu.VMEM((BLOCK, 3 * HD), f32),
            pltpu.VMEM((parts, 3, HALF, HD), bf16),
            pltpu.VMEM((2, HD, HD), bf16),
            pltpu.VMEM((2, BLOCK, HD), bf16),
            pltpu.VMEM((BLOCK, HD), f32),
            pltpu.VMEM((BLOCK, HD), f32),
            pltpu.VMEM((2, 2, RING, RING, HALF, HD), bf16),
            pltpu.VMEM((2, 2, 2, RING // 2, HALF, HD), bf16),
            pltpu.VMEM((2, 2, 2, RING, HALF, HD), bf16),
            pltpu.VMEM((2, 2, RING, HALF, HD), bf16),
            pltpu.VMEM((2, 2, 3, HALF, HD), bf16),
            pltpu.VMEM((2, HALF, HD), bf16),
            pltpu.VMEM((2, HALF, HD), bf16),
            pltpu.VMEM((2, HALF, HD), f32),
            dma((5,)),
            dma,
            dma,
            dma((80,)),
            dma((80,)),
            dma((3 * parts,)),
            dma((3 * parts,)),
            dma((3 * parts,)),
            dma((8,)),
            dma((8,)),
            dma((16,)),
            dma((16,)),
            dma((12,)),
            dma((12,)),
            dma((2,)),
            dma((2,)),
        ],
        compiler_params=pltpu.CompilerParams(collective_id=0, has_side_effects=True),
    )(tokens.reshape(2, HALF, HD), by_kind, out_weight, signs, rows)


def solution(mesh):
    in_specs = (
        P("ctx", "head"),
        P(None, None, "head"),
        P("head", None),
        P("head", None, None),
        P("head", None, None),
    )
    out_specs = P("ctx", "head")
    return jax.shard_map(shards, mesh=mesh, in_specs=in_specs, out_specs=out_specs, check_vma=False)
```
